32 devices in a mesh: inner: 8 (over y, x, core), outer: 4 (over z).
Axes of the slice: x: 2, y: 2, z: 4, core: 2. Of those that a mesh axis runs over, the one named last changes fastest.
Arguments:
- queries: bfloat16 [8192, 4096], P(('outer', 'inner')), may hold values from -2048 to 2048
- keys: bfloat16 [8192, 512], P(('outer', 'inner')), may hold values from -2048 to 2048
- values: bfloat16 [8192, 512], P(('outer', 'inner')), may hold values from -6 to 6
- decays: float32 [4, 8192], P(None, ('outer', 'inner')), may hold values from 0.9 to 1
- query_map: bfloat16 [32, 128, 64], P('inner'), may hold values from -2 to 2
- key_map: bfloat16 [4, 128, 64], replicated, may hold values from -2 to 2
- prefix_state: float32 [4, 128, 128], replicated, may hold values from -384 to 384
- prefix_norm: float32 [4, 128], replicated, may hold values from 4 to 64
Outputs:
- attended: bfloat16 [8192, 4096], P(('outer', 'inner'))
The draws below stay inside these ranges and needn't reach their ends.
All inputs are finite; a program needn't handle non-finite values.
Results may differ from the reference program's by a relative error of at most 0.0075.
Values may be sent and summed in bfloat16 or wider, within the bound.
A program may use at most 64 MiB of HBM per device.

```python
import math
import jax
import jax.numpy as jnp
from jax import lax

HEADS = 32
KV_HEADS = 4
HEAD_DIM = 128
HALF_FEAT = 64
FEATURES = 128
GROUP = 8
TOK_DEV = 256
TOKENS = 8192


def map_values(seed_key, map_count):
    drawn = jax.random.normal(seed_key, (map_count, HEAD_DIM, HALF_FEAT), jnp.float32) * HEAD_DIM ** (-0.5)
    return drawn.astype(jnp.bfloat16)


def draw_query_map(key, part):
    return map_values(jax.random.fold_in(key, 11), HEADS)


def draw_key_map(key, part):
    return map_values(jax.random.fold_in(key, 21), KV_HEADS)


def draw_queries(key, part):
    base = jax.random.normal(jax.random.fold_in(key, 12), (TOKENS, HEADS, HEAD_DIM), jnp.float32)
    return base.reshape(TOKENS, HEADS * HEAD_DIM).astype(jnp.bfloat16)


def draw_keys(key, part):
    base = jax.random.normal(jax.random.fold_in(key, 22), (TOKENS, KV_HEADS, HEAD_DIM), jnp.float32)
    return base.reshape(TOKENS, KV_HEADS * HEAD_DIM).astype(jnp.bfloat16)


def draw_decays(key, part):
    order = jax.random.permutation(jax.random.fold_in(key, 41), KV_HEADS)
    quick = order < KV_HEADS // 2
    quick_draw = jax.random.uniform(jax.random.fold_in(key, 42), (KV_HEADS,), jnp.float32)
    quick_rate = jnp.exp(math.log(1.0 / 60.0) + quick_draw * math.log(1.5))
    slow_draw = jax.random.uniform(jax.random.fold_in(key, 43), (KV_HEADS,), jnp.float32)
    slow_rate = jnp.exp(math.log(0.2) + slow_draw * math.log(3.5)) / TOKENS
    rate = jnp.where(quick, quick_rate, slow_rate)[:, None]
    block_draw = jax.random.uniform(jax.random.fold_in(key, 44), (KV_HEADS, TOKENS // TOK_DEV), jnp.float32)
    block_factor = jnp.repeat(jnp.exp((2.0 * block_draw - 1.0) * math.log(2.0)), TOK_DEV, axis=1)
    token_draw = jax.random.uniform(jax.random.fold_in(key, 45), (KV_HEADS, TOKENS), jnp.float32)
    token_factor = jnp.exp((2.0 * token_draw - 1.0) * math.log(2.0))
    forget_rate = rate * block_factor * token_factor
    starts = jax.random.randint(jax.random.fold_in(key, 46), (KV_HEADS, 3), 0, TOKENS - 3)
    position = jnp.arange(TOKENS)
    token_gap_length = position[None, None, :] - starts[:, :, None]
    token_span = jnp.any((token_gap_length >= 0) & (token_gap_length < 3), axis=1)
    forget_rate = jnp.where(token_span, 0.1, forget_rate)
    return jnp.exp(-forget_rate)


def steps_of(rng, shape, cuts, low, high):
    level = 1.0
    for dim, parts in cuts:
        draws = jax.random.uniform(jax.random.fold_in(jax.random.fold_in(rng, 6), dim), (parts,), jnp.float32, low / len(cuts), high / len(cuts))
        level = level * jnp.repeat(jnp.exp(draws), shape[dim] // parts).reshape((-1,) + (1,) * (len(shape) - 1 - dim))
    return level


def noise(key, shape, deviation, bound, pieces=(), dtype=jnp.bfloat16):
    values = deviation * jax.random.normal(key, shape, jnp.float32)
    if pieces:
        values = values * steps_of(key, shape, pieces, -0.22, 0.18)
    return jnp.clip(values, -bound, bound).astype(dtype)


def setup_inputs(seed: int = 0) -> dict:
    key_list = jax.random.split(jax.random.key(seed), 9)
    queries = draw_queries(jax.random.fold_in(key_list[8], 71), 0)
    keys = draw_keys(jax.random.fold_in(key_list[8], 71), 0)
    values = noise(key_list[2], (TOKENS, KV_HEADS * HEAD_DIM), 1.0, 6.0, ((0, 32),))
    decays = draw_decays(jax.random.fold_in(key_list[8], 71), 0)
    query_map = draw_query_map(jax.random.fold_in(key_list[8], 71), 0)
    key_map = draw_key_map(jax.random.fold_in(key_list[8], 71), 0)
    prefix_state = noise(key_list[6], (KV_HEADS, FEATURES, HEAD_DIM), 64.0, 384.0, (), jnp.float32)
    prefix_norm = jnp.clip(jnp.exp(jax.random.uniform(key_list[7], (KV_HEADS, FEATURES), jnp.float32, math.log(4.0), math.log(64.0))), 4.0, 64.0)
    return dict(queries=queries, keys=keys, values=values, decays=decays, query_map=query_map, key_map=key_map, prefix_state=prefix_state, prefix_norm=prefix_norm)


def features(stacked, weight):
    row_count, head_count, head_width = stacked.shape
    half_width = weight.shape[2]
    both_signs = jnp.concatenate([weight, -weight], axis=2)
    score_matrix = jnp.einsum("tnd,ndf->tnf", stacked.astype(jnp.float32), both_signs.astype(jnp.float32))
    halves = score_matrix.reshape(row_count, head_count, 2, half_width)
    shifted = jnp.exp(halves - jnp.max(halves, axis=3, keepdims=True))
    normed = shifted / jnp.sum(shifted, axis=3, keepdims=True)
    return normed.reshape(row_count, head_count, 2 * half_width).astype(jnp.bfloat16)


def reference(queries, keys, values, decays, query_map, key_map, prefix_state, prefix_norm):
    block_count = TOKENS // TOK_DEV
    query_blocks = queries.reshape(block_count, TOK_DEV, HEADS * HEAD_DIM)
    key_blocks = keys.reshape(block_count, TOK_DEV, KV_HEADS * HEAD_DIM)
    value_blocks = values.reshape(block_count, TOK_DEV, KV_HEADS * HEAD_DIM)
    decay_blocks = jnp.transpose(decays.reshape(KV_HEADS, block_count, TOK_DEV), (1, 0, 2))
    causal = jnp.arange(TOK_DEV)[:, None] >= jnp.arange(TOK_DEV)[None, :]

    def one_block(carried, inputs):
        state_in, norm_in = carried
        q_rows, k_rows, v_rows, d_rows = inputs
        query_feat = features(q_rows.reshape(TOK_DEV, HEADS, HEAD_DIM), query_map)
        key_feature_rows = features(k_rows.reshape(TOK_DEV, KV_HEADS, HEAD_DIM), key_map)
        value_head_rows = v_rows.reshape(TOK_DEV, KV_HEADS, HEAD_DIM).astype(jnp.float32)
        local_log = jnp.cumsum(jnp.log(d_rows), axis=1)
        block_log = local_log[:, -1]
        to_end = jnp.exp(block_log[:, None] - local_log)
        keyed = (key_feature_rows.astype(jnp.float32) * jnp.transpose(to_end)[:, :, None]).astype(jnp.bfloat16)
        keyed_wide = keyed.astype(jnp.float32)
        block_state = jnp.einsum("tgf,tgd->gfd", keyed_wide, value_head_rows)
        block_norm = jnp.sum(keyed_wide, axis=0)
        group_reshaped = query_feat.reshape(TOK_DEV, KV_HEADS, GROUP, FEATURES).astype(jnp.float32)
        score_matrix = jnp.einsum("woya,xoa->oywx", group_reshaped, key_feature_rows.astype(jnp.float32))
        gaps = local_log[:, :, None] - local_log[:, None, :]
        decay_mask = jnp.where(causal[None], jnp.exp(jnp.minimum(gaps, 0.0)), 0.0)
        weights = score_matrix * decay_mask[:, None]
        inner_den = jnp.sum(weights, axis=3)
        rounded_values = weights.astype(jnp.bfloat16).astype(jnp.float32)
        inner_numerator = jnp.einsum("fyko,ofa->kfya", rounded_values, value_head_rows)
        state_half = state_in.astype(jnp.bfloat16).astype(jnp.float32)
        outer_num = jnp.einsum("tgrf,gfd->tgrd", group_reshaped, state_half)
        outer_den = jnp.einsum("tgrf,gf->tgr", group_reshaped, norm_in, precision=lax.Precision.HIGHEST)
        scale = jnp.exp(jnp.transpose(local_log))[:, :, None]
        numer = inner_numerator + scale[..., None] * outer_num
        denom = jnp.transpose(inner_den, (2, 0, 1)) + scale * outer_den
        attended = (numer / denom[..., None]).reshape(TOK_DEV, HEADS * HEAD_DIM).astype(jnp.bfloat16)
        block_decay = jnp.exp(block_log)
        state_out = block_decay[:, None, None] * state_in + block_state
        norm_out = block_decay[:, None] * norm_in + block_norm
        return (state_out, norm_out), attended

    final_carry, attended = lax.scan(one_block, (prefix_state, prefix_norm), (query_blocks, key_blocks, value_blocks, decay_blocks))
    return attended.reshape(TOKENS, HEADS * HEAD_DIM)
```

```python
import functools
import jax
import jax.numpy as jnp
from jax import lax
from jax.experimental import pallas as pl
from jax.experimental.pallas import tpu as pltpu
from jax.sharding import PartitionSpec as P

HEADS = 32
KV_HEADS = 4
HEAD_DIM = 128
HALF = 64
FEATURES = 128
GROUP = 8
TOK = 256
BLK = 128
AUG = 144
F32 = jnp.float32
BF16 = jnp.bfloat16
MESH = pl.DeviceIdType.MESH


def dot(a, b):
    return jnp.dot(a, b, preferred_element_type=F32)


def dot_nt(a, b, precision=None):
    return lax.dot_general(
        a, b, (((1,), (1,)), ((), ())), preferred_element_type=F32, precision=precision
    )


def features_t(u):
    top = jnp.max(u, axis=0, keepdims=True)
    bottom = jnp.min(u, axis=0, keepdims=True)
    pos = jnp.exp(u - top)
    neg = jnp.exp(bottom - u)
    pos = pos * (1.0 / jnp.sum(pos, axis=0, keepdims=True))
    neg = neg * (1.0 / jnp.sum(neg, axis=0, keepdims=True))
    return jnp.concatenate([pos, neg], axis=0).astype(BF16)


def two_parts(norm, decay):
    both = jnp.concatenate([norm, decay], axis=0)
    high = both.astype(BF16).astype(F32)
    return jnp.concatenate([high, both - high], axis=0).astype(BF16)


def unpacked(ref, j, rows, mine):
    parts = ref[j, rows:].astype(F32)
    both = parts[:8] + parts[8:]
    norm, decay = both[:KV_HEADS], both[KV_HEADS:]
    lead = decay[0:1]
    for g in range(1, KV_HEADS):
        lead = jnp.where(mine == g, decay[g : g + 1], lead)
    return ref[j, 0:rows].astype(F32), norm, decay, lead


def kernel(
    n_in, n_out,
    q_hbm, k_hbm, v_hbm, d_hbm, qm_hbm, km_hbm, ps_hbm, pn_hbm, rhs_a, rhs_b, lhs_a, lhs_b,
    q_ref, k_ref, v_ref, d_ref, km_ref, ps_ref, pn_ref, load,
    maps, phik, dm_a, dm_b, prefix_t,
    send1, recv1, send2, recv2, send3, recv3,
    map_s, map_r, s1, r1, s2, r2, s3, r3,
):
    me = lax.axis_index("inner")
    band = lax.axis_index("outer")
    per = HEADS // n_in
    rows = KV_HEADS * HEAD_DIM // n_in

    loads = [
        pltpu.make_async_copy(source, target, load.at[i])
        for i, (source, target) in enumerate((
            (d_hbm, d_ref), (k_hbm, k_ref), (km_hbm, km_ref), (v_hbm, v_ref),
            (qm_hbm, maps.at[me]), (q_hbm, q_ref), (ps_hbm, ps_ref), (pn_hbm, pn_ref),
        ))
    ]
    for copy in loads:
        copy.start()
    barrier = pltpu.get_barrier_semaphore()
    for k in range(1, n_in):
        pl.semaphore_signal(
            barrier, inc=1, device_id={"inner": lax.rem(me + k, n_in)}, device_id_type=MESH
        )
    for k in range(1, n_out):
        pl.semaphore_signal(
            barrier, inc=1, device_id={"outer": lax.rem(band + k, n_out)}, device_id_type=MESH
        )

    chips = n_in // 2
    chip, core = lax.div(me, 2), lax.rem(me, 2)
    sibling = chip * 2 + 1 - core

    def map_copy(c):
        return pltpu.make_async_remote_copy(
            src_ref=maps.at[me], dst_ref=maps.at[me],
            send_sem=map_s.at[2 * c], recv_sem=map_r.at[2 * c],
            device_id={"inner": lax.rem(chip + c, chips) * 2 + core}, device_id_type=MESH,
        )

    def map_pass(c):
        source = lax.rem(chip - c + chips, chips) * 2 + core
        return pltpu.make_async_remote_copy(
            src_ref=maps.at[source], dst_ref=maps.at[source],
            send_sem=map_s.at[2 * c + 1], recv_sem=map_r.at[2 * c + 1],
            device_id={"inner": sibling}, device_id_type=MESH,
        )

    def copy1(k):
        peer = lax.rem(me + k, n_in)
        return pltpu.make_async_remote_copy(
            src_ref=send1.at[peer], dst_ref=recv1.at[me],
            send_sem=s1.at[k], recv_sem=r1.at[k],
            device_id={"inner": peer}, device_id_type=MESH,
        )

    def copy2(k):
        return pltpu.make_async_remote_copy(
            src_ref=send2, dst_ref=recv2.at[band],
            send_sem=s2.at[k], recv_sem=r2.at[k],
            device_id={"outer": lax.rem(band + k, n_out)}, device_id_type=MESH,
        )

    def copy3(k):
        peer = lax.rem(me + k, n_in)
        return pltpu.make_async_remote_copy(
            src_ref=send3.at[peer], dst_ref=recv3.at[me],
            send_sem=s3.at[k], recv_sem=r3.at[k],
            device_id={"inner": peer}, device_id_type=MESH,
        )


    for i in range(4):
        loads[i].wait()
    logs = jnp.log(d_ref[...])
    r = lax.broadcasted_iota(jnp.int32, (TOK, TOK), 0)
    c = lax.broadcasted_iota(jnp.int32, (TOK, TOK), 1)
    lower = jnp.where(c <= r, 1.0, 0.0).astype(F32)
    local_row = dot_nt(logs, lower, lax.Precision.HIGHEST)
    local_col = dot_nt(lower, logs, lax.Precision.HIGHEST)
    last = local_row[:, TOK - 1 :]
    to_end = jnp.exp(last - local_row)
    grow = jnp.exp(-local_col)
    causal = r[:BLK, :BLK] <= c[:BLK, :BLK]
    pad_row = lax.broadcasted_iota(jnp.int32, (AUG - HEAD_DIM, TOK), 0)
    ones_pad = jnp.where(pad_row == 0, 1.0, 0.0).astype(BF16)
    norms = []
    for g in range(KV_HEADS):
        cols = slice(g * HEAD_DIM, (g + 1) * HEAD_DIM)
        u = dot_nt(km_ref[g], k_ref[:, cols])
        feat = features_t(u)
        phik[g] = feat.T
        keyed = (feat.astype(F32) * to_end[g : g + 1]).astype(BF16)
        vt = jnp.concatenate([v_ref[:, cols].T, ones_pad], axis=0)
        lhs_a[g, :, 0:BLK] = vt[:, 0:BLK]
        lhs_b[g] = vt[:, BLK:]
        state = dot_nt(vt, keyed)
        norms.append(state[HEAD_DIM : HEAD_DIM + 1])
        for part in range(HEAD_DIM // rows):
            send1[g * (HEAD_DIM // rows) + part, 0:rows] = (
                state[part * rows : (part + 1) * rows].astype(BF16)
            )
        wide = jnp.broadcast_to(grow[:, g : g + 1], (TOK, BLK))
        dm_a[g, :, 0:BLK] = jnp.where(causal, wide[:BLK], 0.0)
        dm_a[g, :, BLK:] = wide[:BLK]
        dm_b[g] = jnp.where(causal, wide[BLK:], 0.0)
    small = two_parts(
        jnp.concatenate(norms, axis=0), jnp.broadcast_to(jnp.exp(last), (KV_HEADS, FEATURES))
    )
    for j in range(n_in):
        send1[j, rows:] = small
    loads[4].wait()
    pl.semaphore_wait(barrier, n_in + n_out - 2)
    for k in range(1, n_in):
        copy1(k).start()
    for c in range(1, chips):
        map_copy(c).start()
    map_pass(0).start()
    recv1[me] = send1[me]
    for i in range(5, 8):
        loads[i].wait()
    for g in range(KV_HEADS):
        prefix_t[g * HEAD_DIM : (g + 1) * HEAD_DIM] = ps_ref[g].T

    def heads_of(source):
        for i in range(per):
            h = source * per + i
            g = lax.div(h, GROUP)
            q = q_ref[:, pl.ds(pl.multiple_of(h * HEAD_DIM, HEAD_DIM), HEAD_DIM)]
            feat = features_t(dot_nt(maps[source, i], q))
            rhs_a[h, BLK:] = feat
            keys = phik[g]
            rhs_a[h, 0:BLK] = (dot(keys[:BLK], feat) * dm_a[g]).astype(BF16)
            rhs_b[h] = (dot(keys[BLK:], feat[:, BLK:]) * dm_b[g]).astype(BF16)

    def heads_direct(c, carry):
        map_copy(c).wait_recv()
        map_pass(c).start()
        heads_of(lax.rem(chip - c + chips, chips) * 2 + core)
        return carry

    def heads_passed(c, carry):
        map_pass(c).wait_recv()
        heads_of(lax.rem(chip - c + chips, chips) * 2 + 1 - core)
        return carry

    mine = lax.div(me * rows, HEAD_DIM)
    heads_of(me)
    heads_passed(0, 0)

    for k in range(1, n_in):
        copy1(k).wait_recv()
    total = jnp.zeros((rows, FEATURES), F32)
    total_norm = jnp.zeros((KV_HEADS, FEATURES), F32)
    total_decay = jnp.ones((KV_HEADS, FEATURES), F32)
    for j in range(n_in):
        block, block_norm, decay, lead = unpacked(recv1, j, rows, mine)
        total = lead * total + block
        total_norm = decay * total_norm + block_norm
        total_decay = decay * total_decay
    send2[0:rows] = total.astype(BF16)
    send2[rows:] = two_parts(total_norm, total_decay)
    for k in range(1, n_out):
        copy2(k).start()
    recv2[band] = send2[...]

    middle = 1 + (chips - 1) * 2 // 3
    lax.fori_loop(1, middle, heads_direct, 0)

    for k in range(1, n_out):
        copy2(k).wait_recv()
    state = prefix_t[pl.ds(pl.multiple_of(me * rows, rows), rows)]
    norm = pn_ref[...]
    for z in range(n_out - 1):
        before = z < band
        block, block_norm, decay, lead = unpacked(recv2, z, rows, mine)
        state = jnp.where(before, lead * state + block, state)
        norm = jnp.where(before, decay * norm + block_norm, norm)
    my_norm = norm
    for j in range(n_in):
        send3[j] = state.astype(BF16)
        my_norm = jnp.where(j == me, norm, my_norm)
        block, block_norm, decay, lead = unpacked(recv1, j, rows, mine)
        state = lead * state + block
        norm = decay * norm + block_norm
    for k in range(1, n_in):
        copy3(k).start()
    recv3[me] = send3[me]

    lax.fori_loop(middle, chips, heads_direct, 0)
    lax.fori_loop(1, chips, heads_passed, 0)

    high = my_norm.astype(BF16).astype(F32)
    low = my_norm - high
    pick = lax.broadcasted_iota(jnp.int32, (AUG - HEAD_DIM, FEATURES), 0)
    for g in range(KV_HEADS):
        lhs_a[g, HEAD_DIM:, BLK:] = jnp.where(
            pick == 0, high[g : g + 1], jnp.where(pick == 1, low[g : g + 1], 0.0)
        ).astype(BF16)
    for k in range(1, n_in):
        copy3(k).wait_recv()
    for j in range(n_in):
        g, at = divmod(j * rows, HEAD_DIM)
        lhs_a[g, at : at + rows, BLK:] = recv3[j]

    for k in range(1, n_in):
        copy1(k).wait_send()
        copy3(k).wait_send()
    for c in range(1, chips):
        map_copy(c).wait_send()
    for c in range(chips):
        map_pass(c).wait_send()
    for k in range(1, n_out):
        copy2(k).wait_send()


def finish(wide_ref, late_ref, left_ref, left_late_ref, o_hbm, o_ref, drain):
    drains = []
    for g in range(KV_HEADS):
        for h in range(g * GROUP, (g + 1) * GROUP):
            wide = dot(left_ref[g], wide_ref[h])
            late = dot(left_late_ref[g], late_ref[h])
            full = jnp.concatenate([wide[:, :BLK], wide[:, BLK:] + late], axis=1)
            den = full[HEAD_DIM : HEAD_DIM + 1] + full[HEAD_DIM + 1 : HEAD_DIM + 2]
            out = (full[:HEAD_DIM] * (1.0 / den)).astype(BF16)
            o_ref[:, h * HEAD_DIM : (h + 1) * HEAD_DIM] = out.T
        cols = pl.ds(g * GROUP * HEAD_DIM, GROUP * HEAD_DIM)
        drains.append(pltpu.make_async_copy(o_ref.at[:, cols], o_hbm.at[:, cols], drain.at[g]))
        drains[g].start()
    for copy in drains:
        copy.wait()


def per_device(n_in, n_out, q, k, v, d, query_map, key_map, prefix_state, prefix_norm):
    args = (
        q, k, v, d, jnp.swapaxes(query_map, 1, 2), jnp.swapaxes(key_map, 1, 2),
        prefix_state, prefix_norm,
    )
    per = HEADS // n_in
    rows = KV_HEADS * HEAD_DIM // n_in
    dma = pltpu.SemaphoreType.DMA
    wide, late, left, left_late = pl.pallas_call(
        functools.partial(kernel, n_in, n_out),
        out_shape=(
            pltpu.VMEM((HEADS, TOK, TOK), BF16),
            pltpu.VMEM((HEADS, BLK, BLK), BF16),
            pltpu.VMEM((KV_HEADS, AUG, TOK), BF16),
            pltpu.VMEM((KV_HEADS, AUG, BLK), BF16),
        ),
        in_specs=[pl.BlockSpec(memory_space=pltpu.HBM)] * 8,
        out_specs=(pl.BlockSpec(memory_space=pltpu.VMEM),) * 4,
        scratch_shapes=[
            pltpu.VMEM((TOK, HEADS * HEAD_DIM), BF16),
            pltpu.VMEM((TOK, KV_HEADS * HEAD_DIM), BF16),
            pltpu.VMEM((TOK, KV_HEADS * HEAD_DIM), BF16),
            pltpu.VMEM((KV_HEADS, TOK), F32),
            pltpu.VMEM((KV_HEADS, HALF, HEAD_DIM), BF16),
            pltpu.VMEM((KV_HEADS, FEATURES, HEAD_DIM), F32),
            pltpu.VMEM((KV_HEADS, FEATURES), F32),
            dma((8,)),
            pltpu.VMEM((n_in, per, HALF, HEAD_DIM), BF16),
            pltpu.VMEM((KV_HEADS, TOK, FEATURES), BF16),
            pltpu.VMEM((KV_HEADS, BLK, TOK), F32),
            pltpu.VMEM((KV_HEADS, BLK, BLK), F32),
            pltpu.VMEM((KV_HEADS * HEAD_DIM, FEATURES), F32),
            pltpu.VMEM((n_in, rows + 16, FEATURES), BF16),
            pltpu.VMEM((n_in, rows + 16, FEATURES), BF16),
            pltpu.VMEM((rows + 16, FEATURES), BF16),
            pltpu.VMEM((n_out, rows + 16, FEATURES), BF16),
            pltpu.VMEM((n_in, rows, FEATURES), BF16),
            pltpu.VMEM((n_in, rows, FEATURES), BF16),
            dma((n_in,)), dma((n_in,)), dma((n_in,)), dma((n_in,)),
            dma((n_out,)), dma((n_out,)), dma((n_in,)), dma((n_in,)),
        ],
        compiler_params=pltpu.CompilerParams(
            collective_id=0, has_side_effects=True, vmem_limit_bytes=57 << 20
        ),
    )(*args)
    return pl.pallas_call(
        finish,
        out_shape=jax.ShapeDtypeStruct((TOK, HEADS * HEAD_DIM), BF16),
        in_specs=[pl.BlockSpec(memory_space=pltpu.VMEM)] * 4,
        out_specs=pl.BlockSpec(memory_space=pltpu.HBM),
        scratch_shapes=[
            pltpu.VMEM((TOK, HEADS * HEAD_DIM), BF16),
            dma((KV_HEADS,)),
        ],
        compiler_params=pltpu.CompilerParams(vmem_limit_bytes=24 << 20),
    )(wide, late, left, left_late)


def solution(mesh):
    placed = (
        P(("outer", "inner"), None),
        P(("outer", "inner"), None),
        P(("outer", "inner"), None),
        P(None, ("outer", "inner")),
        P("inner", None, None),
        P(),
        P(),
        P(),
    )
    return jax.shard_map(
        functools.partial(per_device, mesh.shape["inner"], mesh.shape["outer"]),
        mesh=mesh,
        in_specs=placed,
        out_specs=P(("outer", "inner"), None),
        check_vma=False,
    )
```

```python
import functools
import jax
import jax.numpy as jnp
from jax import lax
from jax.experimental import pallas as pl
from jax.experimental.pallas import tpu as pltpu
from jax.sharding import PartitionSpec as P

HEADS = 32
KV_HEADS = 4
HEAD_DIM = 128
HALF = 64
FEATURES = 128
GROUP = 8
PAIRS = HEADS // 2
TOK = 256
BLK = 128
AUG = 144
F32 = jnp.float32
BF16 = jnp.bfloat16
MESH = pl.DeviceIdType.MESH


def dot(a, b):
    return jnp.dot(a, b, preferred_element_type=F32)


def dot_nt(a, b):
    return lax.dot_general(a, b, (((1,), (1,)), ((), ())), preferred_element_type=F32)


def features_t(u):
    top = jnp.max(u, axis=0, keepdims=True)
    bottom = jnp.min(u, axis=0, keepdims=True)
    pos = jnp.exp(u - top)
    neg = jnp.exp(bottom - u)
    pos = pos * (1.0 / jnp.sum(pos, axis=0, keepdims=True))
    neg = neg * (1.0 / jnp.sum(neg, axis=0, keepdims=True))
    return jnp.concatenate([pos, neg], axis=0)


def two_parts(norm, decay):
    both = jnp.concatenate([norm, decay], axis=0)
    high = both.astype(BF16).astype(F32)
    return jnp.concatenate([high, both - high], axis=0).astype(BF16)


def unpacked(ref, j, rows, mine):
    parts = ref[j, rows:].astype(F32)
    both = parts[:8] + parts[8:]
    norm, decay = both[:KV_HEADS], both[KV_HEADS:]
    lead = decay[0:1]
    for g in range(1, KV_HEADS):
        lead = jnp.where(mine == g, decay[g : g + 1], lead)
    return ref[j, 0:rows].astype(F32), norm, decay, lead


def flipped(a, k):
    out = a
    bit = 1
    while bit <= k:
        if k & bit:
            out = out + bit - 2 * bit * lax.rem(lax.div(a, bit), 2)
        bit *= 2
    return out


def kernel(
    n_in, n_out,
    q_hbm, k_hbm, v_hbm, d_hbm, qm_hbm, km_hbm, ps_hbm, pn_hbm, rhs, lhs,
    q_ref, k_ref, v_ref, d_ref, km_ref, ps_ref, pn_ref, load,
    maps, keyed, early, mask, scores, prefix_t, within,
    send1, recv1, send2, recv2, send3, recv3,
    map_s, map_r, s1, r1, s2, r2, s3, r3, ready,
):
    me = lax.axis_index("inner")
    band = lax.axis_index("outer")
    per = HEADS // n_in
    rows = KV_HEADS * HEAD_DIM // n_in

    loads = [
        pltpu.make_async_copy(source, target, load.at[i])
        for i, (source, target) in enumerate((
            (d_hbm, d_ref), (k_hbm, k_ref), (km_hbm, km_ref), (v_hbm, v_ref),
            (qm_hbm, maps.at[me]), (q_hbm, q_ref), (ps_hbm, ps_ref), (pn_hbm, pn_ref),
        ))
    ]
    for copy in loads:
        copy.start()
    barrier = pltpu.get_barrier_semaphore()
    for k in range(n_in - 1, 0, -1):
        pl.semaphore_signal(
            barrier, inc=1, device_id={"inner": flipped(me, k)}, device_id_type=MESH
        )

    def greet_later(z, carry):
        pl.semaphore_signal(barrier, inc=1, device_id={"outer": z}, device_id_type=MESH)
        return carry

    lax.fori_loop(band + 1, n_out, greet_later, 0)

    chips = n_in // 2
    chip, core = lax.div(me, 2), lax.rem(me, 2)
    sibling = chip * 2 + 1 - core

    def map_copy(c):
        return pltpu.make_async_remote_copy(
            src_ref=maps.at[me], dst_ref=maps.at[me],
            send_sem=map_s.at[2 * c], recv_sem=map_r.at[2 * c],
            device_id={"inner": lax.rem(chip + c, chips) * 2 + core}, device_id_type=MESH,
        )

    def map_pass(c):
        source = lax.rem(chip - c + chips, chips) * 2 + core
        return pltpu.make_async_remote_copy(
            src_ref=maps.at[source], dst_ref=maps.at[source],
            send_sem=map_s.at[2 * c + 1], recv_sem=map_r.at[2 * c + 1],
            device_id={"inner": sibling}, device_id_type=MESH,
        )

    def copy1(k):
        peer = flipped(me, k)
        return pltpu.make_async_remote_copy(
            src_ref=send1.at[peer], dst_ref=recv1.at[me],
            send_sem=s1.at[k], recv_sem=r1.at[k],
            device_id={"inner": peer}, device_id_type=MESH,
        )

    def copy2(source, target):
        return pltpu.make_async_remote_copy(
            src_ref=send2, dst_ref=recv2.at[source],
            send_sem=s2.at[target], recv_sem=r2.at[source],
            device_id={"outer": target}, device_id_type=MESH,
        )

    def copy3(k):
        peer = flipped(me, k)
        return pltpu.make_async_remote_copy(
            src_ref=send3.at[peer], dst_ref=recv3.at[me],
            send_sem=s3.at[k], recv_sem=r3.at[k],
            device_id={"inner": peer}, device_id_type=MESH,
        )

    r = lax.broadcasted_iota(jnp.int32, (BLK, BLK), 0)
    c = lax.broadcasted_iota(jnp.int32, (BLK, BLK), 1)
    upper = jnp.where(r <= c, 1.0, 0.0).astype(BF16)
    mask[:, 0:BLK] = upper
    mask[:, BLK:] = upper
    pad_row = lax.broadcasted_iota(jnp.int32, (AUG - HEAD_DIM, BLK), 0)
    ones_pad = jnp.where(pad_row == 0, 1.0, 0.0).astype(BF16)
    for g in range(KV_HEADS):
        for half in range(2):
            lhs[g, half, HEAD_DIM:, 0:BLK] = ones_pad

    for i in range(4):
        loads[i].wait()
    logs = jnp.log(d_ref[...])
    split = []
    rest = jnp.concatenate(
        [logs[:, :BLK], logs[:, BLK:]], axis=0
    )
    for _ in range(3):
        part = rest.astype(BF16).astype(F32)
        split.append(part)
        rest = rest - part
    split.append(jnp.zeros_like(rest))
    summed = dot(jnp.concatenate(split, axis=0).astype(BF16), upper)
    local = summed[0:8] + summed[8:16] + summed[16:24]
    grow = jnp.exp(-local)
    closing = jnp.broadcast_to(jnp.exp(local[:, BLK - 1 :]), (2 * KV_HEADS, FEATURES))
    closing_early, closing_late = closing[:KV_HEADS], closing[KV_HEADS:]
    norms = []
    for g in range(KV_HEADS):
        cols = slice(g * HEAD_DIM, (g + 1) * HEAD_DIM)
        feat = features_t(dot_nt(km_ref[g], k_ref[:, cols]))
        vt = v_ref[:, cols].T
        ends = []
        for half in range(2):
            at = slice(half * BLK, (half + 1) * BLK)
            row = half * KV_HEADS + g
            grown = (feat[:, at] * grow[row : row + 1]).astype(BF16).T
            keyed[g, half] = grown
            lhs[g, half, 0:HEAD_DIM, 0:BLK] = vt[:, at]
            left = jnp.concatenate([vt[:, at], ones_pad], axis=0)
            ends.append(dot(left, grown) * closing[row : row + 1])
        early[g] = ends[0]
        state = ends[0] * closing_late[g : g + 1] + ends[1]
        norms.append(state[HEAD_DIM : HEAD_DIM + 1])
        for part in range(HEAD_DIM // rows):
            send1[g * (HEAD_DIM // rows) + part, 0:rows] = (
                state[part * rows : (part + 1) * rows].astype(BF16)
            )
    small = two_parts(jnp.concatenate(norms, axis=0), closing_early * closing_late)
    for j in range(n_in):
        send1[j, rows:] = small
    loads[4].wait()
    pl.semaphore_wait(barrier, n_in - 1 + band)
    for k in range(n_in - 1, 0, -1):
        copy1(k).start()

    def tell_earlier(z, carry):
        pl.semaphore_signal(ready, inc=1, device_id={"outer": z}, device_id_type=MESH)
        return carry

    lax.fori_loop(0, band, tell_earlier, 0)
    for c in range(1, chips):
        map_copy(c).start()
    map_pass(0).start()
    recv1[me] = send1[me]
    for i in range(5, 8):
        loads[i].wait()
    mine = lax.div(me * rows, HEAD_DIM)
    prefix_t[...] = ps_ref[mine].T

    def heads_of(place):
        first = place * per

        def project(i):
            for n in (2 * i, 2 * i + 1):
                h = place * (2 * per) + n
                q = q_ref[:, pl.ds(pl.multiple_of(h * HEAD_DIM, HEAD_DIM), HEAD_DIM)]
                scores[n] = dot_nt(maps[place * 2 + n // per, n % per], q)

        def soften(i):
            for n in (2 * i, 2 * i + 1):
                feat = features_t(scores[n]).astype(BF16)
                at = slice((n % 2) * BLK, (n % 2 + 1) * BLK)
                rhs[first + i, 0, BLK:, at] = feat[:, :BLK]
                rhs[first + i, 1, BLK:, at] = feat[:, BLK:]

        def weigh(i):
            g = lax.div((first + i) * 2, GROUP)
            for half in range(2):
                weights = dot(keyed[g, half], rhs[first + i, half, BLK:])
                rhs[first + i, half, 0:BLK] = weights.astype(BF16) * mask[...]

        project(0)
        for i in range(per + 1):
            if i + 1 < per:
                project(i + 1)
            if i < per:
                soften(i)
            if i > 0:
                weigh(i - 1)

    def heads_later(c, carry):
        map_pass(c).wait_recv()
        heads_of(lax.rem(chip - c + chips, chips))
        return carry

    def pass_on(c, carry):
        map_copy(c).wait_recv()
        map_pass(c).start()
        return carry

    map_pass(0).wait_recv()
    heads_of(chip)

    for k in range(1, n_in):
        copy1(k).wait_recv()
    total = jnp.zeros((rows, FEATURES), F32)
    total_norm = jnp.zeros((KV_HEADS, FEATURES), F32)
    total_decay = jnp.ones((KV_HEADS, FEATURES), F32)
    total_lead = jnp.ones((1, FEATURES), F32)
    leads = []
    my_within = total_norm
    my_decay = total_decay
    for j in range(n_in):
        within[j] = total
        leads.append(total_lead)
        my_within = jnp.where(j == me, total_norm, my_within)
        my_decay = jnp.where(j == me, total_decay, my_decay)
        block, block_norm, decay, lead = unpacked(recv1, j, rows, mine)
        total = lead * total + block
        total_norm = decay * total_norm + block_norm
        total_decay = decay * total_decay
        total_lead = lead * total_lead
    send2[0:rows] = total.astype(BF16)
    send2[rows:] = two_parts(total_norm, total_decay)

    @pl.when(band < n_out - 1)
    def _():
        pl.semaphore_wait(ready, n_out - 1 - band)

    def send_later(z, carry):
        copy2(band, z).start()
        return carry

    lax.fori_loop(band + 1, n_out, send_later, 0)

    lax.fori_loop(1, chips, pass_on, 0)
    lax.fori_loop(1, chips, heads_later, 0)

    def arrived(z, carry):
        copy2(z, z).wait_recv()
        return carry

    lax.fori_loop(0, band, arrived, 0)
    state = prefix_t[pl.ds(pl.multiple_of(lax.rem(me * rows, HEAD_DIM), rows), rows)]
    norm = pn_ref[...]
    for z in range(n_out - 1):
        before = z < band
        block, block_norm, decay, lead = unpacked(recv2, z, rows, mine)
        state = jnp.where(before, lead * state + block, state)
        norm = jnp.where(before, decay * norm + block_norm, norm)
    for j in range(n_in):
        send3[j] = (leads[j] * state + within[j]).astype(BF16)
    for k in range(n_in - 1, 0, -1):
        copy3(k).start()
    recv3[me] = send3[me]
    my_norm = my_decay * norm + my_within

    mid_norm = closing_early * my_norm + jnp.concatenate(
        [early[g, HEAD_DIM : HEAD_DIM + 1] for g in range(KV_HEADS)], axis=0
    )
    pick = lax.broadcasted_iota(jnp.int32, (AUG - HEAD_DIM, FEATURES), 0)
    for half, entry in enumerate((my_norm, mid_norm)):
        high = entry.astype(BF16).astype(F32)
        low = entry - high
        for g in range(KV_HEADS):
            lhs[g, half, HEAD_DIM:, BLK:] = jnp.where(
                pick == 0, high[g : g + 1], jnp.where(pick == 1, low[g : g + 1], 0.0)
            ).astype(BF16)
    for k in range(1, n_in):
        copy3(k).wait_recv()
    for j in range(n_in):
        g, at = divmod(j * rows, HEAD_DIM)
        entry = recv3[j]
        lhs[g, 0, at : at + rows, BLK:] = entry
        lhs[g, 1, at : at + rows, BLK:] = (
            closing_early[g : g + 1] * entry.astype(F32) + early[g, at : at + rows]
        ).astype(BF16)

    for k in range(1, n_in):
        copy1(k).wait_send()
        copy3(k).wait_send()
    for c in range(1, chips):
        map_copy(c).wait_send()
    for c in range(chips):
        map_pass(c).wait_send()

    def sent(z, carry):
        copy2(band, z).wait_send()
        return carry

    lax.fori_loop(band + 1, n_out, sent, 0)


def finish(rhs_ref, lhs_ref, o_hbm, o_ref, drain):
    drains = []
    for pair in range(PAIRS):
        g = pair * 2 // GROUP
        for half in range(2):
            full = dot(lhs_ref[g, half], rhs_ref[pair, half])
            den = full[HEAD_DIM : HEAD_DIM + 1] + full[HEAD_DIM + 1 : HEAD_DIM + 2]
            out = (full[:HEAD_DIM] * (1.0 / den)).astype(BF16)
            for i in range(2):
                h = pair * 2 + i
                o_ref[half * BLK : (half + 1) * BLK, h * HEAD_DIM : (h + 1) * HEAD_DIM] = (
                    out[:, i * BLK : (i + 1) * BLK].T
                )
        if (pair + 1) * 2 % GROUP == 0:
            cols = pl.ds(g * GROUP * HEAD_DIM, GROUP * HEAD_DIM)
            drains.append(pltpu.make_async_copy(o_ref.at[:, cols], o_hbm.at[:, cols], drain.at[g]))
            drains[g].start()
    for copy in drains:
        copy.wait()


def per_device(n_in, n_out, q, k, v, d, query_map, key_map, prefix_state, prefix_norm):
    args = (
        q, k, v, d, jnp.swapaxes(query_map, 1, 2), jnp.swapaxes(key_map, 1, 2),
        prefix_state, prefix_norm,
    )
    per = HEADS // n_in
    rows = KV_HEADS * HEAD_DIM // n_in
    dma = pltpu.SemaphoreType.DMA
    rhs, lhs = pl.pallas_call(
        functools.partial(kernel, n_in, n_out),
        out_shape=(
            pltpu.VMEM((PAIRS, 2, TOK, TOK), BF16),
            pltpu.VMEM((KV_HEADS, 2, AUG, TOK), BF16),
        ),
        in_specs=[pl.BlockSpec(memory_space=pltpu.HBM)] * 8,
        out_specs=(pl.BlockSpec(memory_space=pltpu.VMEM),) * 2,
        scratch_shapes=[
            pltpu.VMEM((TOK, HEADS * HEAD_DIM), BF16),
            pltpu.VMEM((TOK, KV_HEADS * HEAD_DIM), BF16),
            pltpu.VMEM((TOK, KV_HEADS * HEAD_DIM), BF16),
            pltpu.VMEM((KV_HEADS, TOK), F32),
            pltpu.VMEM((KV_HEADS, HALF, HEAD_DIM), BF16),
            pltpu.VMEM((KV_HEADS, FEATURES, HEAD_DIM), F32),
            pltpu.VMEM((KV_HEADS, FEATURES), F32),
            dma((8,)),
            pltpu.VMEM((n_in, per, HALF, HEAD_DIM), BF16),
            pltpu.VMEM((KV_HEADS, 2, BLK, FEATURES), BF16),
            pltpu.VMEM((KV_HEADS, AUG, FEATURES), F32),
            pltpu.VMEM((BLK, TOK), BF16),
            pltpu.VMEM((2 * per, HALF, TOK), F32),
            pltpu.VMEM((HEAD_DIM, FEATURES), F32),
            pltpu.VMEM((n_in, rows, FEATURES), F32),
            pltpu.VMEM((n_in, rows + 16, FEATURES), BF16),
            pltpu.VMEM((n_in, rows + 16, FEATURES), BF16),
            pltpu.VMEM((rows + 16, FEATURES), BF16),
            pltpu.VMEM((n_out, rows + 16, FEATURES), BF16),
            pltpu.VMEM((n_in, rows, FEATURES), BF16),
            pltpu.VMEM((n_in, rows, FEATURES), BF16),
            dma((n_in,)), dma((n_in,)), dma((n_in,)), dma((n_in,)),
            dma((n_out,)), dma((n_out,)), dma((n_in,)), dma((n_in,)),
            pltpu.SemaphoreType.REGULAR,
        ],
        compiler_params=pltpu.CompilerParams(
            collective_id=0, has_side_effects=True, vmem_limit_bytes=57 << 20
        ),
    )(*args)
    return pl.pallas_call(
        finish,
        out_shape=jax.ShapeDtypeStruct((TOK, HEADS * HEAD_DIM), BF16),
        in_specs=[pl.BlockSpec(memory_space=pltpu.VMEM)] * 2,
        out_specs=pl.BlockSpec(memory_space=pltpu.HBM),
        scratch_shapes=[
            pltpu.VMEM((TOK, HEADS * HEAD_DIM), BF16),
            dma((KV_HEADS,)),
        ],
        compiler_params=pltpu.CompilerParams(vmem_limit_bytes=24 << 20),
    )(rhs, lhs)


def solution(mesh):
    placed = (
        P(("outer", "inner"), None),
        P(("outer", "inner"), None),
        P(("outer", "inner"), None),
        P(None, ("outer", "inner")),
        P("inner", None, None),
        P(),
        P(),
        P(),
    )
    return jax.shard_map(
        functools.partial(per_device, mesh.shape["inner"], mesh.shape["outer"]),
        mesh=mesh,
        in_specs=placed,
        out_specs=P(("outer", "inner"), None),
        check_vma=False,
    )
```

```python
import functools
import jax
import jax.numpy as jnp
from jax import lax
from jax.experimental import pallas as pl
from jax.experimental.pallas import tpu as pltpu
from jax.sharding import PartitionSpec as P

HEADS = 32
KV_HEADS = 4
HEAD_DIM = 128
HALF = 64
FEATURES = 128
GROUP = 8
PAIRS = HEADS // 2
TOK = 256
BLK = 128
AUG = 144
F32 = jnp.float32
BF16 = jnp.bfloat16
MESH = pl.DeviceIdType.MESH


def dot(a, b):
    return jnp.dot(a, b, preferred_element_type=F32)


def dot_nt(a, b):
    return lax.dot_general(a, b, (((1,), (1,)), ((), ())), preferred_element_type=F32)


def features_t(u):
    top = jnp.max(u, axis=0, keepdims=True)
    bottom = jnp.min(u, axis=0, keepdims=True)
    pos = jnp.exp(u - top)
    neg = jnp.exp(bottom - u)
    pos = pos * (1.0 / jnp.sum(pos, axis=0, keepdims=True))
    neg = neg * (1.0 / jnp.sum(neg, axis=0, keepdims=True))
    return jnp.concatenate([pos, neg], axis=0)


def two_parts(norm, decay):
    both = jnp.concatenate([norm, decay], axis=0)
    high = both.astype(BF16).astype(F32)
    return jnp.concatenate([high, both - high], axis=0).astype(BF16)


def unpacked(ref, j, rows, mine):
    parts = ref[j, rows:].astype(F32)
    both = parts[:8] + parts[8:]
    norm, decay = both[:KV_HEADS], both[KV_HEADS:]
    lead = decay[0:1]
    for g in range(1, KV_HEADS):
        lead = jnp.where(mine == g, decay[g : g + 1], lead)
    return ref[j, 0:rows].astype(F32), norm, decay, lead


def flipped(a, k):
    out = a
    bit = 1
    while bit <= k:
        if k & bit:
            out = out + bit - 2 * bit * lax.rem(lax.div(a, bit), 2)
        bit *= 2
    return out


def kernel(
    n_in, n_out,
    q_hbm, k_hbm, v_hbm, d_hbm, qm_hbm, km_hbm, ps_hbm, pn_hbm, rhs, lhs,
    q_ref, k_ref, v_ref, d_ref, km_ref, ps_ref, pn_ref, load,
    maps, keyed, early, mask, scores, prefix_t, within,
    send1, recv1, send2, recv2, send3, recv3,
    map_s, map_r, s1, r1, s2, r2, s3, r3, ready,
):
    me = lax.axis_index("inner")
    band = lax.axis_index("outer")
    per = HEADS // n_in
    rows = KV_HEADS * HEAD_DIM // n_in

    loads = [
        pltpu.make_async_copy(source, target, load.at[i])
        for i, (source, target) in enumerate((
            (d_hbm, d_ref), (k_hbm, k_ref), (km_hbm, km_ref), (v_hbm, v_ref),
            (qm_hbm, maps.at[me]), (q_hbm, q_ref), (ps_hbm, ps_ref), (pn_hbm, pn_ref),
        ))
    ]
    for copy in loads:
        copy.start()
    barrier = pltpu.get_barrier_semaphore()
    for k in range(n_in - 1, 0, -1):
        pl.semaphore_signal(
            barrier, inc=1, device_id={"inner": flipped(me, k)}, device_id_type=MESH
        )

    def greet_later(z, carry):
        pl.semaphore_signal(barrier, inc=1, device_id={"outer": z}, device_id_type=MESH)
        return carry

    lax.fori_loop(band + 1, n_out, greet_later, 0)

    chips = n_in // 2
    chip, core = lax.div(me, 2), lax.rem(me, 2)
    sibling = chip * 2 + 1 - core

    def map_copy(c):
        return pltpu.make_async_remote_copy(
            src_ref=maps.at[me], dst_ref=maps.at[me],
            send_sem=map_s, recv_sem=map_r.at[2 * c],
            device_id={"inner": lax.rem(chip + c, chips) * 2 + core}, device_id_type=MESH,
        )

    def map_pass(c):
        source = lax.rem(chip - c + chips, chips) * 2 + core
        return pltpu.make_async_remote_copy(
            src_ref=maps.at[source], dst_ref=maps.at[source],
            send_sem=map_s, recv_sem=map_r.at[2 * c + 1],
            device_id={"inner": sibling}, device_id_type=MESH,
        )

    def copy1(k):
        peer = flipped(me, k)
        return pltpu.make_async_remote_copy(
            src_ref=send1.at[peer], dst_ref=recv1.at[me],
            send_sem=s1, recv_sem=r1,
            device_id={"inner": peer}, device_id_type=MESH,
        )

    def copy2(source, target):
        return pltpu.make_async_remote_copy(
            src_ref=send2, dst_ref=recv2.at[source],
            send_sem=s2.at[target], recv_sem=r2.at[source],
            device_id={"outer": target}, device_id_type=MESH,
        )

    def copy3(k):
        peer = flipped(me, k)
        return pltpu.make_async_remote_copy(
            src_ref=send3.at[peer], dst_ref=recv3.at[me],
            send_sem=s3, recv_sem=r3,
            device_id={"inner": peer}, device_id_type=MESH,
        )

    others = pl.ds(0, n_in - 1)

    def all1():
        return pltpu.make_async_remote_copy(
            src_ref=send1.at[others], dst_ref=recv1.at[others], send_sem=s1, recv_sem=r1,
            device_id={"inner": sibling}, device_id_type=MESH,
        )

    def all3():
        return pltpu.make_async_remote_copy(
            src_ref=send3.at[others], dst_ref=recv3.at[others], send_sem=s3, recv_sem=r3,
            device_id={"inner": sibling}, device_id_type=MESH,
        )

    def all_maps():
        return pltpu.make_async_remote_copy(
            src_ref=maps.at[others], dst_ref=maps.at[others], send_sem=map_s, recv_sem=map_r.at[0],
            device_id={"inner": sibling}, device_id_type=MESH,
        )

    r = lax.broadcasted_iota(jnp.int32, (BLK, BLK), 0)
    c = lax.broadcasted_iota(jnp.int32, (BLK, BLK), 1)
    upper = jnp.where(r <= c, 1.0, 0.0).astype(BF16)
    mask[:, 0:BLK] = upper
    mask[:, BLK:] = upper
    pad_row = lax.broadcasted_iota(jnp.int32, (AUG - HEAD_DIM, BLK), 0)
    ones_pad = jnp.where(pad_row == 0, 1.0, 0.0).astype(BF16)
    for g in range(KV_HEADS):
        for half in range(2):
            lhs[g, half, HEAD_DIM:, 0:BLK] = ones_pad

    for i in range(3):
        loads[i].wait()
    logs = jnp.log(d_ref[...])
    split = []
    rest = jnp.concatenate([logs[:, :BLK], logs[:, BLK:]], axis=0)
    for _ in range(3):
        part = rest.astype(BF16).astype(F32)
        split.append(part)
        rest = rest - part
    split.append(jnp.zeros_like(rest))
    summed = dot(jnp.concatenate(split, axis=0).astype(BF16), upper)
    for g in range(KV_HEADS):
        scores[g] = dot_nt(km_ref[g], k_ref[:, g * HEAD_DIM : (g + 1) * HEAD_DIM])
    local = summed[0:8] + summed[8:16] + summed[16:24]
    grow = jnp.exp(-local)
    closing = jnp.broadcast_to(jnp.exp(local[:, BLK - 1 :]), (2 * KV_HEADS, FEATURES))
    closing_early, closing_late = closing[:KV_HEADS], closing[KV_HEADS:]
    loads[3].wait()
    for g in range(KV_HEADS):
        vt = v_ref[:, g * HEAD_DIM : (g + 1) * HEAD_DIM].T
        for half in range(2):
            lhs[g, half, 0:HEAD_DIM, 0:BLK] = vt[:, half * BLK : (half + 1) * BLK]
    for g in range(KV_HEADS):
        feat = features_t(scores[g])
        for half in range(2):
            row = half * KV_HEADS + g
            grown = feat[:, half * BLK : (half + 1) * BLK] * grow[row : row + 1]
            keyed[g, half] = grown.astype(BF16).T
    norms = []
    for g in range(KV_HEADS):
        ends = [
            dot(lhs[g, half, :, 0:BLK], keyed[g, half])
            * closing[half * KV_HEADS + g : half * KV_HEADS + g + 1]
            for half in range(2)
        ]
        early[g] = ends[0]
        state = ends[0] * closing_late[g : g + 1] + ends[1]
        norms.append(state[HEAD_DIM : HEAD_DIM + 1])
        for part in range(HEAD_DIM // rows):
            send1[g * (HEAD_DIM // rows) + part, 0:rows] = (
                state[part * rows : (part + 1) * rows].astype(BF16)
            )
    small = two_parts(jnp.concatenate(norms, axis=0), closing_early * closing_late)
    for j in range(n_in):
        send1[j, rows:] = small
    loads[4].wait()
    pl.semaphore_wait(barrier, n_in - 1 + band)
    for k in range(n_in - 1, 0, -1):
        copy1(k).start()

    def tell_earlier(z, carry):
        pl.semaphore_signal(ready, inc=1, device_id={"outer": z}, device_id_type=MESH)
        return carry

    lax.fori_loop(0, band, tell_earlier, 0)
    for c in range(1, chips):
        map_copy(c).start()
    map_pass(0).start()
    recv1[me] = send1[me]
    for i in range(5, 8):
        loads[i].wait()
    mine = lax.div(me * rows, HEAD_DIM)
    prefix_t[...] = ps_ref[mine].T

    def heads_of(place):
        first = place * per

        def project(i):
            for n in (2 * i, 2 * i + 1):
                h = place * (2 * per) + n
                q = q_ref[:, pl.ds(pl.multiple_of(h * HEAD_DIM, HEAD_DIM), HEAD_DIM)]
                scores[n] = dot_nt(maps[place * 2 + n // per, n % per], q)

        def soften(i):
            for n in (2 * i, 2 * i + 1):
                feat = features_t(scores[n]).astype(BF16)
                at = slice((n % 2) * BLK, (n % 2 + 1) * BLK)
                rhs[first + i, 0, BLK:, at] = feat[:, :BLK]
                rhs[first + i, 1, BLK:, at] = feat[:, BLK:]

        def weigh(i):
            g = lax.div((first + i) * 2, GROUP)
            for half in range(2):
                weights = dot(keyed[g, half], rhs[first + i, half, BLK:])
                rhs[first + i, half, 0:BLK] = weights.astype(BF16) * mask[...]

        project(0)
        for i in range(per + 1):
            if i + 1 < per:
                project(i + 1)
            if i < per:
                soften(i)
            if i > 0:
                weigh(i - 1)

    def heads_later(c, carry):
        map_pass(c).wait_recv()
        heads_of(lax.rem(chip - c + chips, chips))
        return carry

    def pass_on(c, carry):
        map_copy(c).wait_recv()
        map_pass(c).start()
        return carry

    map_pass(0).wait_recv()
    heads_of(chip)

    all1().wait_recv()
    total = jnp.zeros((rows, FEATURES), F32)
    total_norm = jnp.zeros((KV_HEADS, FEATURES), F32)
    total_decay = jnp.ones((KV_HEADS, FEATURES), F32)
    total_lead = jnp.ones((1, FEATURES), F32)
    leads = []
    my_within = total_norm
    my_decay = total_decay
    for j in range(n_in):
        within[j] = total
        leads.append(total_lead)
        my_within = jnp.where(j == me, total_norm, my_within)
        my_decay = jnp.where(j == me, total_decay, my_decay)
        block, block_norm, decay, lead = unpacked(recv1, j, rows, mine)
        total = lead * total + block
        total_norm = decay * total_norm + block_norm
        total_decay = decay * total_decay
        total_lead = lead * total_lead
    send2[0:rows] = total.astype(BF16)
    send2[rows:] = two_parts(total_norm, total_decay)

    @pl.when(band < n_out - 1)
    def _():
        pl.semaphore_wait(ready, n_out - 1 - band)

    def send_later(z, carry):
        copy2(band, z).start()
        return carry

    lax.fori_loop(band + 1, n_out, send_later, 0)

    def send_states(state):
        for j in range(n_in):
            send3[j] = (leads[j] * state + within[j]).astype(BF16)
        for k in range(n_in - 1, 0, -1):
            copy3(k).start()
        recv3[me] = send3[me]

    my_prefix = pl.ds(pl.multiple_of(lax.rem(me * rows, HEAD_DIM), rows), rows)

    @pl.when(band == 0)
    def _():
        send_states(prefix_t[my_prefix])

    lax.fori_loop(1, chips, pass_on, 0)
    lax.fori_loop(1, 2, heads_later, 0)

    def arrived(z, carry):
        copy2(z, z).wait_recv()
        return carry

    lax.fori_loop(0, band, arrived, 0)
    state = prefix_t[my_prefix]
    norm = pn_ref[...]
    for z in range(n_out - 1):
        before = z < band
        block, block_norm, decay, lead = unpacked(recv2, z, rows, mine)
        state = jnp.where(before, lead * state + block, state)
        norm = jnp.where(before, decay * norm + block_norm, norm)

    @pl.when(band > 0)
    def _():
        send_states(state)

    lax.fori_loop(2, chips, heads_later, 0)
    my_norm = my_decay * norm + my_within

    mid_norm = closing_early * my_norm + jnp.concatenate(
        [early[g, HEAD_DIM : HEAD_DIM + 1] for g in range(KV_HEADS)], axis=0
    )
    pick = lax.broadcasted_iota(jnp.int32, (AUG - HEAD_DIM, FEATURES), 0)
    for half, entry in enumerate((my_norm, mid_norm)):
        high = entry.astype(BF16).astype(F32)
        low = entry - high
        for g in range(KV_HEADS):
            lhs[g, half, HEAD_DIM:, BLK:] = jnp.where(
                pick == 0, high[g : g + 1], jnp.where(pick == 1, low[g : g + 1], 0.0)
            ).astype(BF16)
    all3().wait_recv()
    for j in range(n_in):
        g, at = divmod(j * rows, HEAD_DIM)
        entry = recv3[j]
        lhs[g, 0, at : at + rows, BLK:] = entry
        lhs[g, 1, at : at + rows, BLK:] = (
            closing_early[g : g + 1] * entry.astype(F32) + early[g, at : at + rows]
        ).astype(BF16)

    all1().wait_send()
    all3().wait_send()
    all_maps().wait_send()

    def sent(z, carry):
        copy2(band, z).wait_send()
        return carry

    lax.fori_loop(band + 1, n_out, sent, 0)


def finish(rhs_ref, lhs_ref, o_hbm, o_ref, drain):
    drains = []
    for pair in range(PAIRS):
        g = pair * 2 // GROUP
        for half in range(2):
            full = dot(lhs_ref[g, half], rhs_ref[pair, half])
            den = full[HEAD_DIM : HEAD_DIM + 1] + full[HEAD_DIM + 1 : HEAD_DIM + 2]
            out = (full[:HEAD_DIM] * (1.0 / den)).astype(BF16)
            for i in range(2):
                h = pair * 2 + i
                o_ref[half * BLK : (half + 1) * BLK, h * HEAD_DIM : (h + 1) * HEAD_DIM] = (
                    out[:, i * BLK : (i + 1) * BLK].T
                )
        cols = pl.ds(pair * 2 * HEAD_DIM, 2 * HEAD_DIM)
        drains.append(pltpu.make_async_copy(o_ref.at[:, cols], o_hbm.at[:, cols], drain.at[pair]))
        drains[pair].start()
    for copy in drains:
        copy.wait()


def per_device(n_in, n_out, q, k, v, d, query_map, key_map, prefix_state, prefix_norm):
    args = (
        q, k, v, d, jnp.swapaxes(query_map, 1, 2), jnp.swapaxes(key_map, 1, 2),
        prefix_state, prefix_norm,
    )
    per = HEADS // n_in
    rows = KV_HEADS * HEAD_DIM // n_in
    dma = pltpu.SemaphoreType.DMA
    rhs, lhs = pl.pallas_call(
        functools.partial(kernel, n_in, n_out),
        out_shape=(
            pltpu.VMEM((PAIRS, 2, TOK, TOK), BF16),
            pltpu.VMEM((KV_HEADS, 2, AUG, TOK), BF16),
        ),
        in_specs=[pl.BlockSpec(memory_space=pltpu.HBM)] * 8,
        out_specs=(pl.BlockSpec(memory_space=pltpu.VMEM),) * 2,
        scratch_shapes=[
            pltpu.VMEM((TOK, HEADS * HEAD_DIM), BF16),
            pltpu.VMEM((TOK, KV_HEADS * HEAD_DIM), BF16),
            pltpu.VMEM((TOK, KV_HEADS * HEAD_DIM), BF16),
            pltpu.VMEM((KV_HEADS, TOK), F32),
            pltpu.VMEM((KV_HEADS, HALF, HEAD_DIM), BF16),
            pltpu.VMEM((KV_HEADS, FEATURES, HEAD_DIM), F32),
            pltpu.VMEM((KV_HEADS, FEATURES), F32),
            dma((8,)),
            pltpu.VMEM((n_in, per, HALF, HEAD_DIM), BF16),
            pltpu.VMEM((KV_HEADS, 2, BLK, FEATURES), BF16),
            pltpu.VMEM((KV_HEADS, AUG, FEATURES), F32),
            pltpu.VMEM((BLK, TOK), BF16),
            pltpu.VMEM((max(2 * per, KV_HEADS), HALF, TOK), F32),
            pltpu.VMEM((HEAD_DIM, FEATURES), F32),
            pltpu.VMEM((n_in, rows, FEATURES), F32),
            pltpu.VMEM((n_in, rows + 16, FEATURES), BF16),
            pltpu.VMEM((n_in, rows + 16, FEATURES), BF16),
            pltpu.VMEM((rows + 16, FEATURES), BF16),
            pltpu.VMEM((n_out, rows + 16, FEATURES), BF16),
            pltpu.VMEM((n_in, rows, FEATURES), BF16),
            pltpu.VMEM((n_in, rows, FEATURES), BF16),
            dma(()), dma((n_in,)), dma(()), dma(()),
            dma((n_out,)), dma((n_out,)), dma(()), dma(()),
            pltpu.SemaphoreType.REGULAR,
        ],
        compiler_params=pltpu.CompilerParams(
            collective_id=0, has_side_effects=True, vmem_limit_bytes=57 << 20
        ),
    )(*args)
    return pl.pallas_call(
        finish,
        out_shape=jax.ShapeDtypeStruct((TOK, HEADS * HEAD_DIM), BF16),
        in_specs=[pl.BlockSpec(memory_space=pltpu.VMEM)] * 2,
        out_specs=pl.BlockSpec(memory_space=pltpu.HBM),
        scratch_shapes=[
            pltpu.VMEM((TOK, HEADS * HEAD_DIM), BF16),
            dma((PAIRS,)),
        ],
        compiler_params=pltpu.CompilerParams(vmem_limit_bytes=24 << 20),
    )(rhs, lhs)


def solution(mesh):
    placed = (
        P(("outer", "inner"), None),
        P(("outer", "inner"), None),
        P(("outer", "inner"), None),
        P(None, ("outer", "inner")),
        P("inner", None, None),
        P(),
        P(),
        P(),
    )
    return jax.shard_map(
        functools.partial(per_device, mesh.shape["inner"], mesh.shape["outer"]),
        mesh=mesh,
        in_specs=placed,
        out_specs=P(("outer", "inner"), None),
        check_vma=False,
    )
```

```python
import functools
import jax
import jax.numpy as jnp
from jax import lax
from jax.experimental import pallas as pl
from jax.experimental.pallas import tpu as pltpu
from jax.sharding import PartitionSpec as P

HEADS = 32
KV_HEADS = 4
HEAD_DIM = 128
HALF = 64
FEATURES = 128
GROUP = 8
PAIRS = HEADS // 2
TOK = 256
BLK = 128
AUG = 144
F32 = jnp.float32
BF16 = jnp.bfloat16
MESH = pl.DeviceIdType.MESH


def dot(a, b):
    return jnp.dot(a, b, preferred_element_type=F32)


def dot_nt(a, b):
    return lax.dot_general(a, b, (((1,), (1,)), ((), ())), preferred_element_type=F32)


def features_t(u):
    top = jnp.max(u, axis=0, keepdims=True)
    bottom = jnp.min(u, axis=0, keepdims=True)
    pos = jnp.exp(u - top)
    neg = jnp.exp(bottom - u)
    pos = pos * (1.0 / jnp.sum(pos, axis=0, keepdims=True))
    neg = neg * (1.0 / jnp.sum(neg, axis=0, keepdims=True))
    return jnp.concatenate([pos, neg], axis=0)


def two_parts(norm, decay):
    both = jnp.concatenate([norm, decay], axis=0)
    high = both.astype(BF16).astype(F32)
    return jnp.concatenate([high, both - high], axis=0).astype(BF16)


def unpacked(ref, j, rows, mine):
    parts = ref[j, rows:].astype(F32)
    both = parts[:8] + parts[8:]
    norm, decay = both[:KV_HEADS], both[KV_HEADS:]
    lead = decay[0:1]
    for g in range(1, KV_HEADS):
        lead = jnp.where(mine == g, decay[g : g + 1], lead)
    return ref[j, 0:rows].astype(F32), norm, decay, lead


def flipped(a, k):
    out = a
    bit = 1
    while bit <= k:
        if k & bit:
            out = out + bit - 2 * bit * lax.rem(lax.div(a, bit), 2)
        bit *= 2
    return out


def kernel(
    n_in, n_out,
    q_hbm, k_hbm, v_hbm, d_hbm, qm_hbm, km_hbm, ps_hbm, pn_hbm, rhs, lhs,
    q_ref, k_ref, v_ref, d_ref, km_ref, ps_ref, pn_ref, load,
    maps, keyed, early, mask, scores, prefix_t, within,
    send1, recv1, send2, recv2, send3, recv3,
    map_s, map_r, s1, r1, s2, r2, s3, r3, ready,
):
    me = lax.axis_index("inner")
    band = lax.axis_index("outer")
    per = HEADS // n_in
    rows = KV_HEADS * HEAD_DIM // n_in

    loads = [
        pltpu.make_async_copy(source, target, load.at[i])
        for i, (source, target) in enumerate((
            (d_hbm, d_ref), (k_hbm, k_ref), (km_hbm, km_ref), (v_hbm, v_ref),
            (qm_hbm, maps.at[me]), (q_hbm, q_ref), (ps_hbm, ps_ref), (pn_hbm, pn_ref),
        ))
    ]
    for copy in loads:
        copy.start()
    barrier = pltpu.get_barrier_semaphore()
    for k in range(n_in - 1, 0, -1):
        pl.semaphore_signal(
            barrier, inc=1, device_id={"inner": flipped(me, k)}, device_id_type=MESH
        )

    def greet_later(z, carry):
        pl.semaphore_signal(barrier, inc=1, device_id={"outer": z}, device_id_type=MESH)
        return carry

    lax.fori_loop(band + 1, n_out, greet_later, 0)

    chips = n_in // 2
    chip, core = lax.div(me, 2), lax.rem(me, 2)
    sibling = chip * 2 + 1 - core

    def map_copy(c):
        return pltpu.make_async_remote_copy(
            src_ref=maps.at[me], dst_ref=maps.at[me],
            send_sem=map_s, recv_sem=map_r.at[2 * c],
            device_id={"inner": lax.rem(chip + c, chips) * 2 + core}, device_id_type=MESH,
        )

    def map_pass(c):
        source = lax.rem(chip - c + chips, chips) * 2 + core
        return pltpu.make_async_remote_copy(
            src_ref=maps.at[source], dst_ref=maps.at[source],
            send_sem=map_s, recv_sem=map_r.at[2 * c + 1],
            device_id={"inner": sibling}, device_id_type=MESH,
        )

    def copy1(k):
        peer = flipped(me, k)
        return pltpu.make_async_remote_copy(
            src_ref=send1.at[peer], dst_ref=recv1.at[me],
            send_sem=s1, recv_sem=r1,
            device_id={"inner": peer}, device_id_type=MESH,
        )

    def copy2(source, target):
        return pltpu.make_async_remote_copy(
            src_ref=send2, dst_ref=recv2.at[source],
            send_sem=s2.at[target], recv_sem=r2.at[source],
            device_id={"outer": target}, device_id_type=MESH,
        )

    def copy3(k):
        peer = flipped(me, k)
        return pltpu.make_async_remote_copy(
            src_ref=send3.at[peer], dst_ref=recv3.at[me],
            send_sem=s3, recv_sem=r3,
            device_id={"inner": peer}, device_id_type=MESH,
        )

    others = pl.ds(0, n_in - 1)

    def all1():
        return pltpu.make_async_remote_copy(
            src_ref=send1.at[others], dst_ref=recv1.at[others], send_sem=s1, recv_sem=r1,
            device_id={"inner": sibling}, device_id_type=MESH,
        )

    def all3():
        return pltpu.make_async_remote_copy(
            src_ref=send3.at[others], dst_ref=recv3.at[others], send_sem=s3, recv_sem=r3,
            device_id={"inner": sibling}, device_id_type=MESH,
        )

    def all_maps():
        return pltpu.make_async_remote_copy(
            src_ref=maps.at[others], dst_ref=maps.at[others], send_sem=map_s, recv_sem=map_r.at[0],
            device_id={"inner": sibling}, device_id_type=MESH,
        )

    r = lax.broadcasted_iota(jnp.int32, (BLK, BLK), 0)
    c = lax.broadcasted_iota(jnp.int32, (BLK, BLK), 1)
    upper = jnp.where(r <= c, 1.0, 0.0).astype(BF16)
    mask[:, 0:BLK] = upper
    mask[:, BLK:] = upper
    pad_row = lax.broadcasted_iota(jnp.int32, (AUG - HEAD_DIM, BLK), 0)
    ones_pad = jnp.where(pad_row == 0, 1.0, 0.0).astype(BF16)
    for g in range(KV_HEADS):
        for half in range(2):
            lhs[g, half, HEAD_DIM:, 0:BLK] = ones_pad

    for i in range(3):
        loads[i].wait()
    logs = jnp.log(d_ref[...])
    split = []
    rest = jnp.concatenate([logs[:, :BLK], logs[:, BLK:]], axis=0)
    for _ in range(3):
        part = rest.astype(BF16).astype(F32)
        split.append(part)
        rest = rest - part
    split.append(jnp.zeros_like(rest))
    summed = dot(jnp.concatenate(split, axis=0).astype(BF16), upper)
    for g in range(KV_HEADS):
        scores[g] = dot_nt(km_ref[g], k_ref[:, g * HEAD_DIM : (g + 1) * HEAD_DIM])
    local = summed[0:8] + summed[8:16] + summed[16:24]
    grow = jnp.exp(-local)
    closing = jnp.broadcast_to(jnp.exp(local[:, BLK - 1 :]), (2 * KV_HEADS, FEATURES))
    closing_early, closing_late = closing[:KV_HEADS], closing[KV_HEADS:]
    loads[3].wait()
    for g in range(KV_HEADS):
        vt = v_ref[:, g * HEAD_DIM : (g + 1) * HEAD_DIM].T
        for half in range(2):
            lhs[g, half, 0:HEAD_DIM, 0:BLK] = vt[:, half * BLK : (half + 1) * BLK]
    for g in range(KV_HEADS):
        feat = features_t(scores[g])
        for half in range(2):
            row = half * KV_HEADS + g
            grown = feat[:, half * BLK : (half + 1) * BLK] * grow[row : row + 1]
            keyed[g, half] = grown.astype(BF16).T
    norms = []
    for g in range(KV_HEADS):
        ends = [
            dot(lhs[g, half, :, 0:BLK], keyed[g, half])
            * closing[half * KV_HEADS + g : half * KV_HEADS + g + 1]
            for half in range(2)
        ]
        early[g] = ends[0]
        state = ends[0] * closing_late[g : g + 1] + ends[1]
        norms.append(state[HEAD_DIM : HEAD_DIM + 1])
        for part in range(HEAD_DIM // rows):
            send1[g * (HEAD_DIM // rows) + part, 0:rows] = (
                state[part * rows : (part + 1) * rows].astype(BF16)
            )
    small = two_parts(jnp.concatenate(norms, axis=0), closing_early * closing_late)
    for j in range(n_in):
        send1[j, rows:] = small
    loads[4].wait()
    pl.semaphore_wait(barrier, n_in - 1 + band)
    for k in range(n_in - 1, 0, -1):
        copy1(k).start()

    def tell_earlier(z, carry):
        pl.semaphore_signal(ready, inc=1, device_id={"outer": z}, device_id_type=MESH)
        return carry

    lax.fori_loop(0, band, tell_earlier, 0)
    for c in range(1, chips):
        map_copy(c).start()
    map_pass(0).start()
    recv1[me] = send1[me]
    for i in range(5, 8):
        loads[i].wait()
    mine = lax.div(me * rows, HEAD_DIM)
    prefix_t[...] = ps_ref[mine].T

    def heads_of(place):
        first = place * per

        def project(i):
            for n in (2 * i, 2 * i + 1):
                h = place * (2 * per) + n
                q = q_ref[:, pl.ds(pl.multiple_of(h * HEAD_DIM, HEAD_DIM), HEAD_DIM)]
                scores[n] = dot_nt(maps[place * 2 + n // per, n % per], q)

        def soften(i):
            for n in (2 * i, 2 * i + 1):
                feat = features_t(scores[n]).astype(BF16)
                at = slice((n % 2) * BLK, (n % 2 + 1) * BLK)
                rhs[first + i, 0, BLK:, at] = feat[:, :BLK]
                rhs[first + i, 1, BLK:, at] = feat[:, BLK:]

        def weigh(i):
            g = lax.div((first + i) * 2, GROUP)
            for half in range(2):
                weights = dot(keyed[g, half], rhs[first + i, half, BLK:])
                rhs[first + i, half, 0:BLK] = weights.astype(BF16) * mask[...]

        project(0)
        for i in range(per + 1):
            if i + 1 < per:
                project(i + 1)
            if i < per:
                soften(i)
            if i > 0:
                weigh(i - 1)

    def heads_later(c, carry):
        map_pass(c).wait_recv()
        heads_of(lax.rem(chip - c + chips, chips))
        return carry

    def pass_on(c, carry):
        map_copy(c).wait_recv()
        map_pass(c).start()
        return carry

    map_pass(0).wait_recv()
    heads_of(chip)

    all1().wait_recv()
    total = jnp.zeros((rows, FEATURES), F32)
    total_norm = jnp.zeros((KV_HEADS, FEATURES), F32)
    total_decay = jnp.ones((KV_HEADS, FEATURES), F32)
    total_lead = jnp.ones((1, FEATURES), F32)
    leads = []
    my_within = total_norm
    my_decay = total_decay
    for j in range(n_in):
        within[j] = total
        leads.append(total_lead)
        my_within = jnp.where(j == me, total_norm, my_within)
        my_decay = jnp.where(j == me, total_decay, my_decay)
        block, block_norm, decay, lead = unpacked(recv1, j, rows, mine)
        total = lead * total + block
        total_norm = decay * total_norm + block_norm
        total_decay = decay * total_decay
        total_lead = lead * total_lead
    send2[0:rows] = total.astype(BF16)
    send2[rows:] = two_parts(total_norm, total_decay)

    @pl.when(band < n_out - 1)
    def _():
        pl.semaphore_wait(ready, n_out - 1 - band)

    def send_later(z, carry):
        copy2(band, z).start()
        return carry

    lax.fori_loop(band + 1, n_out, send_later, 0)

    def send_states(state):
        for j in range(n_in):
            send3[j] = (leads[j] * state + within[j]).astype(BF16)
        for k in range(n_in - 1, 0, -1):
            copy3(k).start()
        recv3[me] = send3[me]

    my_prefix = pl.ds(pl.multiple_of(lax.rem(me * rows, HEAD_DIM), rows), rows)

    @pl.when(band == 0)
    def _():
        send_states(prefix_t[my_prefix])

    lax.fori_loop(1, chips, pass_on, 0)

    def arrived(z, carry):
        copy2(z, z).wait_recv()
        return carry

    lax.fori_loop(0, band, arrived, 0)
    state = prefix_t[my_prefix]
    norm = pn_ref[...]
    for z in range(n_out - 1):
        before = z < band
        block, block_norm, decay, lead = unpacked(recv2, z, rows, mine)
        state = jnp.where(before, lead * state + block, state)
        norm = jnp.where(before, decay * norm + block_norm, norm)

    @pl.when(band > 0)
    def _():
        send_states(state)

    lax.fori_loop(1, chips, heads_later, 0)
    my_norm = my_decay * norm + my_within

    mid_norm = closing_early * my_norm + jnp.concatenate(
        [early[g, HEAD_DIM : HEAD_DIM + 1] for g in range(KV_HEADS)], axis=0
    )
    pick = lax.broadcasted_iota(jnp.int32, (AUG - HEAD_DIM, FEATURES), 0)
    for half, entry in enumerate((my_norm, mid_norm)):
        high = entry.astype(BF16).astype(F32)
        low = entry - high
        for g in range(KV_HEADS):
            lhs[g, half, HEAD_DIM:, BLK:] = jnp.where(
                pick == 0, high[g : g + 1], jnp.where(pick == 1, low[g : g + 1], 0.0)
            ).astype(BF16)
    all3().wait_recv()
    for j in range(n_in):
        g, at = divmod(j * rows, HEAD_DIM)
        entry = recv3[j]
        lhs[g, 0, at : at + rows, BLK:] = entry
        lhs[g, 1, at : at + rows, BLK:] = (
            closing_early[g : g + 1] * entry.astype(F32) + early[g, at : at + rows]
        ).astype(BF16)

    all1().wait_send()
    all3().wait_send()
    all_maps().wait_send()

    def sent(z, carry):
        copy2(band, z).wait_send()
        return carry

    lax.fori_loop(band + 1, n_out, sent, 0)


def finish(rhs_ref, lhs_ref, o_hbm, o_ref, drain):
    for pair in range(PAIRS):
        g = pair * 2 // GROUP
        for half in range(2):
            full = dot(lhs_ref[g, half], rhs_ref[pair, half])
            den = full[HEAD_DIM : HEAD_DIM + 1] + full[HEAD_DIM + 1 : HEAD_DIM + 2]
            out = (full[:HEAD_DIM] * (1.0 / den)).astype(BF16)
            for i in range(2):
                h = pair * 2 + i
                o_ref[half * BLK : (half + 1) * BLK, h * HEAD_DIM : (h + 1) * HEAD_DIM] = (
                    out[:, i * BLK : (i + 1) * BLK].T
                )
        cols = pl.ds(pair * 2 * HEAD_DIM, 2 * HEAD_DIM)
        pltpu.make_async_copy(o_ref.at[:, cols], o_hbm.at[:, cols], drain).start()
    pltpu.make_async_copy(o_ref, o_hbm, drain).wait()


def per_device(n_in, n_out, q, k, v, d, query_map, key_map, prefix_state, prefix_norm):
    args = (
        q, k, v, d, jnp.swapaxes(query_map, 1, 2), jnp.swapaxes(key_map, 1, 2),
        prefix_state, prefix_norm,
    )
    per = HEADS // n_in
    rows = KV_HEADS * HEAD_DIM // n_in
    dma = pltpu.SemaphoreType.DMA
    rhs, lhs = pl.pallas_call(
        functools.partial(kernel, n_in, n_out),
        out_shape=(
            pltpu.VMEM((PAIRS, 2, TOK, TOK), BF16),
            pltpu.VMEM((KV_HEADS, 2, AUG, TOK), BF16),
        ),
        in_specs=[pl.BlockSpec(memory_space=pltpu.HBM)] * 8,
        out_specs=(pl.BlockSpec(memory_space=pltpu.VMEM),) * 2,
        scratch_shapes=[
            pltpu.VMEM((TOK, HEADS * HEAD_DIM), BF16),
            pltpu.VMEM((TOK, KV_HEADS * HEAD_DIM), BF16),
            pltpu.VMEM((TOK, KV_HEADS * HEAD_DIM), BF16),
            pltpu.VMEM((KV_HEADS, TOK), F32),
            pltpu.VMEM((KV_HEADS, HALF, HEAD_DIM), BF16),
            pltpu.VMEM((KV_HEADS, FEATURES, HEAD_DIM), F32),
            pltpu.VMEM((KV_HEADS, FEATURES), F32),
            dma((8,)),
            pltpu.VMEM((n_in, per, HALF, HEAD_DIM), BF16),
            pltpu.VMEM((KV_HEADS, 2, BLK, FEATURES), BF16),
            pltpu.VMEM((KV_HEADS, AUG, FEATURES), F32),
            pltpu.VMEM((BLK, TOK), BF16),
            pltpu.VMEM((max(2 * per, KV_HEADS), HALF, TOK), F32),
            pltpu.VMEM((HEAD_DIM, FEATURES), F32),
            pltpu.VMEM((n_in, rows, FEATURES), F32),
            pltpu.VMEM((n_in, rows + 16, FEATURES), BF16),
            pltpu.VMEM((n_in, rows + 16, FEATURES), BF16),
            pltpu.VMEM((rows + 16, FEATURES), BF16),
            pltpu.VMEM((n_out, rows + 16, FEATURES), BF16),
            pltpu.VMEM((n_in, rows, FEATURES), BF16),
            pltpu.VMEM((n_in, rows, FEATURES), BF16),
            dma(()), dma((n_in,)), dma(()), dma(()),
            dma((n_out,)), dma((n_out,)), dma(()), dma(()),
            pltpu.SemaphoreType.REGULAR,
        ],
        compiler_params=pltpu.CompilerParams(
            collective_id=0, has_side_effects=True, vmem_limit_bytes=57 << 20
        ),
    )(*args)
    return pl.pallas_call(
        finish,
        out_shape=jax.ShapeDtypeStruct((TOK, HEADS * HEAD_DIM), BF16),
        in_specs=[pl.BlockSpec(memory_space=pltpu.VMEM)] * 2,
        out_specs=pl.BlockSpec(memory_space=pltpu.HBM),
        scratch_shapes=[
            pltpu.VMEM((TOK, HEADS * HEAD_DIM), BF16),
            dma(()),
        ],
        compiler_params=pltpu.CompilerParams(vmem_limit_bytes=24 << 20),
    )(rhs, lhs)


def solution(mesh):
    placed = (
        P(("outer", "inner"), None),
        P(("outer", "inner"), None),
        P(("outer", "inner"), None),
        P(None, ("outer", "inner")),
        P("inner", None, None),
        P(),
        P(),
        P(),
    )
    return jax.shard_map(
        functools.partial(per_device, mesh.shape["inner"], mesh.shape["outer"]),
        mesh=mesh,
        in_specs=placed,
        out_specs=P(("outer", "inner"), None),
        check_vma=False,
    )
```

```python
import functools
import jax
import jax.numpy as jnp
from jax import lax
from jax.experimental import pallas as pl
from jax.experimental.pallas import tpu as pltpu
from jax.sharding import PartitionSpec as P

HEADS = 32
KV_HEADS = 4
HEAD_DIM = 128
HALF = 64
FEATURES = 128
GROUP = 8
PAIRS = HEADS // 2
TOK = 256
BLK = 128
AUG = 144
F32 = jnp.float32
BF16 = jnp.bfloat16
MESH = pl.DeviceIdType.MESH


def dot(a, b):
    return jnp.dot(a, b, preferred_element_type=F32)


def dot_nt(a, b):
    return lax.dot_general(a, b, (((1,), (1,)), ((), ())), preferred_element_type=F32)


def features_t(u, scale=1.0):
    top = jnp.max(u, axis=0, keepdims=True)
    bottom = jnp.min(u, axis=0, keepdims=True)
    pos = jnp.exp(u - top)
    neg = jnp.exp(bottom - u)
    pos = pos * (scale / jnp.sum(pos, axis=0, keepdims=True))
    neg = neg * (scale / jnp.sum(neg, axis=0, keepdims=True))
    return jnp.concatenate([pos, neg], axis=0)


def two_parts(norm, decay):
    both = jnp.concatenate([norm, decay], axis=0)
    high = both.astype(BF16).astype(F32)
    return jnp.concatenate([high, both - high], axis=0).astype(BF16)


def unpacked(ref, j, rows, mine):
    parts = ref[j, rows:].astype(F32)
    both = parts[:8] + parts[8:]
    norm, decay = both[:KV_HEADS], both[KV_HEADS:]
    lead = decay[0:1]
    for g in range(1, KV_HEADS):
        lead = jnp.where(mine == g, decay[g : g + 1], lead)
    return ref[j, 0:rows].astype(F32), norm, decay, lead


def flipped(a, k):
    out = a
    bit = 1
    while bit <= k:
        if k & bit:
            out = out + bit - 2 * bit * lax.rem(lax.div(a, bit), 2)
        bit *= 2
    return out


def kernel(
    n_in, n_out,
    q_hbm, k_hbm, v_hbm, d_hbm, qm_hbm, km_hbm, ps_hbm, pn_hbm, rhs, lhs, done,
    q_ref, k_ref, v_ref, d_ref, km_ref, ps_ref, pn_ref, load,
    maps, keyed, early, mask, scores, prefix_t, within,
    send1, recv1, send2, recv2, send3, recv3,
    map_s, map_r, s1, r1, s2, r2, s3, r3, near, ready,
):
    me = lax.axis_index("inner")
    band = lax.axis_index("outer")
    per = HEADS // n_in
    rows = KV_HEADS * HEAD_DIM // n_in

    loads = [
        pltpu.make_async_copy(source, target, load.at[i])
        for i, (source, target) in enumerate((
            (d_hbm, d_ref), (k_hbm, k_ref), (km_hbm, km_ref), (v_hbm, v_ref),
            (qm_hbm, maps.at[me]), (q_hbm, q_ref), (ps_hbm, ps_ref), (pn_hbm, pn_ref),
        ))
    ]
    for copy in loads[:5]:
        copy.start()
    barrier = pltpu.get_barrier_semaphore()
    for k in range(n_in - 1, 0, -1):
        pl.semaphore_signal(
            barrier, inc=1, device_id={"inner": flipped(me, k)}, device_id_type=MESH
        )

    def greet_later(z, carry):
        pl.semaphore_signal(barrier, inc=1, device_id={"outer": z}, device_id_type=MESH)
        return carry

    lax.fori_loop(band + 1, n_out, greet_later, 0)

    chips = n_in // 2
    chip, core = lax.div(me, 2), lax.rem(me, 2)
    sibling = chip * 2 + 1 - core

    def map_copy(c):
        return pltpu.make_async_remote_copy(
            src_ref=maps.at[me], dst_ref=maps.at[me],
            send_sem=map_s, recv_sem=map_r.at[2 * c],
            device_id={"inner": lax.rem(chip + c, chips) * 2 + core}, device_id_type=MESH,
        )

    def map_pass(c):
        source = lax.rem(chip - c + chips, chips) * 2 + core
        return pltpu.make_async_remote_copy(
            src_ref=maps.at[source], dst_ref=maps.at[source],
            send_sem=map_s, recv_sem=map_r.at[2 * c + 1],
            device_id={"inner": sibling}, device_id_type=MESH,
        )

    def copy1(k):
        peer = flipped(me, k)
        return pltpu.make_async_remote_copy(
            src_ref=send1.at[peer], dst_ref=recv1.at[me],
            send_sem=s1, recv_sem=r1,
            device_id={"inner": peer}, device_id_type=MESH,
        )

    def copy2(source, target):
        return pltpu.make_async_remote_copy(
            src_ref=send2, dst_ref=recv2.at[source],
            send_sem=s2.at[target], recv_sem=r2.at[source],
            device_id={"outer": target}, device_id_type=MESH,
        )

    def copy3(k):
        peer = flipped(me, k)
        return pltpu.make_async_remote_copy(
            src_ref=send3.at[peer], dst_ref=recv3.at[me],
            send_sem=s3, recv_sem=near if k == 1 else r3,
            device_id={"inner": peer}, device_id_type=MESH,
        )

    others = pl.ds(0, n_in - 1)

    def all1():
        return pltpu.make_async_remote_copy(
            src_ref=send1.at[others], dst_ref=recv1.at[others], send_sem=s1, recv_sem=r1,
            device_id={"inner": sibling}, device_id_type=MESH,
        )

    def all3():
        return pltpu.make_async_remote_copy(
            src_ref=send3.at[others], dst_ref=recv3.at[others], send_sem=s3, recv_sem=r3,
            device_id={"inner": sibling}, device_id_type=MESH,
        )

    def far3():
        return pltpu.make_async_remote_copy(
            src_ref=send3.at[pl.ds(0, n_in - 2)], dst_ref=recv3.at[pl.ds(0, n_in - 2)],
            send_sem=s3, recv_sem=r3, device_id={"inner": sibling}, device_id_type=MESH,
        )

    def all_maps():
        return pltpu.make_async_remote_copy(
            src_ref=maps.at[others], dst_ref=maps.at[others], send_sem=map_s, recv_sem=map_r.at[0],
            device_id={"inner": sibling}, device_id_type=MESH,
        )

    r = lax.broadcasted_iota(jnp.int32, (BLK, BLK), 0)
    c = lax.broadcasted_iota(jnp.int32, (BLK, BLK), 1)
    upper = jnp.where(r <= c, 1.0, 0.0).astype(BF16)
    mask[:, 0:BLK] = upper
    mask[:, BLK:] = upper
    pad_row = lax.broadcasted_iota(jnp.int32, (AUG - HEAD_DIM, BLK), 0)
    ones_pad = jnp.where(pad_row == 0, 1.0, 0.0).astype(BF16)
    for g in range(KV_HEADS):
        for half in range(2):
            lhs[g, half, HEAD_DIM:, 0:BLK] = ones_pad

    for i in range(3):
        loads[i].wait()
    logs = jnp.log(d_ref[...])
    split = []
    rest = jnp.concatenate([logs[:, :BLK], logs[:, BLK:]], axis=0)
    for _ in range(3):
        part = rest.astype(BF16).astype(F32)
        split.append(part)
        rest = rest - part
    split.append(jnp.zeros_like(rest))
    summed = dot(jnp.concatenate(split, axis=0).astype(BF16), upper)
    for g in range(KV_HEADS):
        scores[g] = dot_nt(km_ref[g], k_ref[:, g * HEAD_DIM : (g + 1) * HEAD_DIM])
    local = summed[0:8] + summed[8:16] + summed[16:24]
    late = local[KV_HEADS:, BLK - 1 :]
    whole = local[:KV_HEADS, BLK - 1 :] + late
    to_end = jnp.exp(jnp.concatenate([whole, late], axis=0) - local)
    closing = jnp.broadcast_to(jnp.exp(whole), (KV_HEADS, FEATURES))
    loads[3].wait()
    for copy in loads[5:]:
        copy.start()
    for g in range(KV_HEADS):
        vt = v_ref[:, g * HEAD_DIM : (g + 1) * HEAD_DIM].T
        for half in range(2):
            lhs[g, half, 0:HEAD_DIM, 0:BLK] = vt[:, half * BLK : (half + 1) * BLK]
    for g in range(KV_HEADS):
        scale = jnp.concatenate([to_end[g : g + 1], to_end[KV_HEADS + g : KV_HEADS + g + 1]], axis=1)
        keyed[g] = features_t(scores[g], scale).astype(BF16).T
    norms = []
    for g in range(KV_HEADS):
        left = jnp.concatenate([lhs[g, 0, :, 0:BLK], lhs[g, 1, :, 0:BLK]], axis=1)
        state = dot(left, keyed[g])
        norms.append(state[HEAD_DIM : HEAD_DIM + 1])
        for part in range(HEAD_DIM // rows):
            send1[g * (HEAD_DIM // rows) + part, 0:rows] = (
                state[part * rows : (part + 1) * rows].astype(BF16)
            )
    small = two_parts(jnp.concatenate(norms, axis=0), closing)
    for j in range(n_in):
        send1[j, rows:] = small
    loads[4].wait()
    pl.semaphore_wait(barrier, n_in - 1 + band)
    for k in range(n_in - 1, 0, -1):
        copy1(k).start()

    def tell_earlier(z, carry):
        pl.semaphore_signal(ready, inc=1, device_id={"outer": z}, device_id_type=MESH)
        return carry

    lax.fori_loop(0, band, tell_earlier, 0)

    @pl.when(band == 0)
    def _():
        for c in range(1, chips):
            map_copy(c).start()

    map_pass(0).start()
    recv1[me] = send1[me]
    for g in range(KV_HEADS):
        early[g] = dot(lhs[g, 0, :, 0:BLK], keyed[g, 0:BLK])
    for i in range(5, 8):
        loads[i].wait()
    mine = lax.div(me * rows, HEAD_DIM)
    prefix_t[...] = ps_ref[mine].T

    def run_pairs(pairs):
        def project(n):
            pair, places = pairs[n]
            for e in range(2):
                h = pair * 2 + e
                q = q_ref[:, pl.ds(pl.multiple_of(h * HEAD_DIM, HEAD_DIM), HEAD_DIM)]
                source, i = places[e]
                scores[2 * n + e] = dot_nt(maps[source, i], q)

        def soften(n):
            pair = pairs[n][0]
            for e in range(2):
                feat = features_t(scores[2 * n + e]).astype(BF16)
                at = slice(e * BLK, (e + 1) * BLK)
                rhs[pair, 0, BLK:, at] = feat[:, :BLK]
                rhs[pair, 1, BLK:, at] = feat[:, BLK:]

        def weigh(n):
            pair = pairs[n][0]
            g = lax.div(pair * 2, GROUP)
            for half in range(2):
                keys = keyed[g, half * BLK : (half + 1) * BLK]
                weights = dot(keys, rhs[pair, half, BLK:])
                rhs[pair, half, 0:BLK] = weights.astype(BF16) * mask[...]

        count = len(pairs)
        project(0)
        for n in range(count + 1):
            if n + 1 < count:
                project(n + 1)
            if n < count:
                soften(n)
            if n > 0:
                weigh(n - 1)

    def heads_of(place):
        run_pairs([
            (
                place * per + n,
                [(place * 2 + m // per, m % per) for m in (2 * n, 2 * n + 1)],
            )
            for n in range(per)
        ])

    def heads_from(sources):
        run_pairs([
            (source * (per // 2) + n, [(source, 2 * n), (source, 2 * n + 1)])
            for source in sources
            for n in range(per // 2)
        ])

    def heads_later(c, carry):
        map_pass(c).wait_recv()
        heads_of(lax.rem(chip - c + chips, chips))
        return carry

    def pass_on(c, carry):
        map_copy(c).wait_recv()
        map_pass(c).start()
        return carry

    map_pass(0).wait_recv()
    heads_of(chip)

    @pl.when(band > 0)
    def _():
        for c in range(1, chips):
            map_copy(c).start()


    all1().wait_recv()
    total = jnp.zeros((rows, FEATURES), F32)
    total_norm = jnp.zeros((KV_HEADS, FEATURES), F32)
    total_decay = jnp.ones((KV_HEADS, FEATURES), F32)
    total_lead = jnp.ones((1, FEATURES), F32)
    leads = []
    my_within = total_norm
    my_decay = total_decay
    for j in range(n_in):
        block, block_norm, decay, lead = unpacked(recv1, j, rows, mine)
        total, total_norm = lead * total, decay * total_norm
        total_lead, total_decay = lead * total_lead, decay * total_decay
        within[j] = total
        leads.append(total_lead)
        my_within = jnp.where(j == me, total_norm, my_within)
        my_decay = jnp.where(j == me, total_decay, my_decay)
        total, total_norm = total + block, total_norm + block_norm
    send2[0:rows] = total.astype(BF16)
    send2[rows:] = two_parts(total_norm, total_decay)

    @pl.when(band < n_out - 1)
    def _():
        pl.semaphore_wait(ready, n_out - 1 - band)

    def send_later(z, carry):
        copy2(band, z).start()
        return carry

    lax.fori_loop(band + 1, n_out, send_later, 0)

    def send_states(state):
        for j in range(n_in):
            send3[j] = (leads[j] * state + within[j]).astype(BF16)
        for k in range(n_in - 1, 0, -1):
            copy3(k).start()
        recv3[me] = send3[me]

    my_prefix = pl.ds(pl.multiple_of(lax.rem(me * rows, HEAD_DIM), rows), rows)

    @pl.when(band == 0)
    def _():
        send_states(prefix_t[my_prefix])

    lax.fori_loop(1, chips, pass_on, 0)

    def arrived(z, carry):
        copy2(z, z).wait_recv()
        return carry

    lax.fori_loop(0, band, arrived, 0)
    state = prefix_t[my_prefix]
    norm = pn_ref[...]
    for z in range(n_out - 1):
        before = z < band
        block, block_norm, decay, lead = unpacked(recv2, z, rows, mine)
        state = jnp.where(before, lead * state + block, state)
        norm = jnp.where(before, decay * norm + block_norm, norm)

    @pl.when(band > 0)
    def _():
        send_states(state)

    my_norm = my_decay * norm + my_within

    mid_norm = my_norm + jnp.concatenate(
        [early[g, HEAD_DIM : HEAD_DIM + 1] for g in range(KV_HEADS)], axis=0
    )
    pick = lax.broadcasted_iota(jnp.int32, (AUG - HEAD_DIM, FEATURES), 0)
    for half, entry in enumerate((my_norm, mid_norm)):
        high = entry.astype(BF16).astype(F32)
        low = entry - high
        for g in range(KV_HEADS):
            lhs[g, half, HEAD_DIM:, BLK:] = jnp.where(
                pick == 0, high[g : g + 1], jnp.where(pick == 1, low[g : g + 1], 0.0)
            ).astype(BF16)
    def finish_own():
        copy3(1).wait_recv()
        if chips == KV_HEADS:
            for part in range(2):
                at = slice(part * rows, (part + 1) * rows)
                entry = recv3[chip * 2 + part]
                lhs[chip, 0, at, BLK:] = entry
                lhs[chip, 1, at, BLK:] = (entry.astype(F32) + early[chip, at]).astype(BF16)
            for i in range(GROUP // 2):
                for half in range(2):
                    attend(
                        lhs[chip, half], rhs[chip * (GROUP // 2) + i, half],
                        done, half, i * 2 * HEAD_DIM,
                    )

    def heads_by_device():
        places = [lax.rem(chip - c + chips, chips) for c in range(1, chips)]
        heads_from([place * 2 + core for place in places])
        for c in range(1, chips):
            map_pass(c).wait_recv()
        heads_from([place * 2 + 1 - core for place in places])

    @pl.when(band == 0)
    def _():
        finish_own()
        lax.fori_loop(1, chips, heads_later, 0)

    @pl.when(band > 0)
    def _():
        if per % 2 == 0 and chips <= 4:
            heads_by_device()
        else:
            lax.fori_loop(1, chips, heads_later, 0)
        finish_own()

    far3().wait_recv()
    for j in range(n_in):
        g, at = divmod(j * rows, HEAD_DIM)
        entry = recv3[j]
        lhs[g, 0, at : at + rows, BLK:] = entry
        lhs[g, 1, at : at + rows, BLK:] = (
            entry.astype(F32) + early[g, at : at + rows]
        ).astype(BF16)

    all1().wait_send()
    all3().wait_send()
    all_maps().wait_send()

    def sent(z, carry):
        copy2(band, z).wait_send()
        return carry

    lax.fori_loop(band + 1, n_out, sent, 0)


def attend(left, right, out_ref, half, column):
    full = dot(left, right)
    den = full[HEAD_DIM : HEAD_DIM + 1] + full[HEAD_DIM + 1 : HEAD_DIM + 2]
    out = (full[:HEAD_DIM] * (1.0 / den)).astype(BF16)
    for i in range(2):
        at = column + i * HEAD_DIM
        out_ref[half * BLK : (half + 1) * BLK, at : at + HEAD_DIM] = (
            out[:, i * BLK : (i + 1) * BLK].T
        )


def finish(ready_made, rhs_ref, lhs_ref, done_ref, o_hbm, o_ref, drain, drain_done):
    wide = GROUP * HEAD_DIM
    left_over = KV_HEADS
    own = 0
    if ready_made:
        left_over = KV_HEADS - 1
        own = lax.div(lax.axis_index("inner"), 2)
        early_out = pltpu.make_async_copy(
            done_ref, o_hbm.at[:, pl.ds(pl.multiple_of(own * wide, wide), wide)], drain_done
        )
        early_out.start()
    for n in range(left_over):
        g = lax.rem(own + 1 + n, KV_HEADS)
        for i in range(GROUP // 2):
            column = n * wide + i * 2 * HEAD_DIM
            for half in range(2):
                attend(lhs_ref[g, half], rhs_ref[g * (GROUP // 2) + i, half], o_ref, half, column)
            target = pl.multiple_of(g * wide + i * 2 * HEAD_DIM, 2 * HEAD_DIM)
            pltpu.make_async_copy(
                o_ref.at[:, pl.ds(column, 2 * HEAD_DIM)],
                o_hbm.at[:, pl.ds(target, 2 * HEAD_DIM)], drain,
            ).start()
    pltpu.make_async_copy(
        o_ref.at[:, pl.ds(0, left_over * wide)], o_hbm.at[:, pl.ds(0, left_over * wide)], drain
    ).wait()
    if ready_made:
        early_out.wait()


def per_device(n_in, n_out, q, k, v, d, query_map, key_map, prefix_state, prefix_norm):
    args = (
        q, k, v, d, jnp.swapaxes(query_map, 1, 2), jnp.swapaxes(key_map, 1, 2),
        prefix_state, prefix_norm,
    )
    per = HEADS // n_in
    rows = KV_HEADS * HEAD_DIM // n_in
    dma = pltpu.SemaphoreType.DMA
    rhs, lhs, done = pl.pallas_call(
        functools.partial(kernel, n_in, n_out),
        out_shape=(
            pltpu.VMEM((PAIRS, 2, TOK, TOK), BF16),
            pltpu.VMEM((KV_HEADS, 2, AUG, TOK), BF16),
            pltpu.VMEM((TOK, GROUP * HEAD_DIM), BF16),
        ),
        in_specs=[pl.BlockSpec(memory_space=pltpu.HBM)] * 8,
        out_specs=(pl.BlockSpec(memory_space=pltpu.VMEM),) * 3,
        scratch_shapes=[
            pltpu.VMEM((TOK, HEADS * HEAD_DIM), BF16),
            pltpu.VMEM((TOK, KV_HEADS * HEAD_DIM), BF16),
            pltpu.VMEM((TOK, KV_HEADS * HEAD_DIM), BF16),
            pltpu.VMEM((KV_HEADS, TOK), F32),
            pltpu.VMEM((KV_HEADS, HALF, HEAD_DIM), BF16),
            pltpu.VMEM((KV_HEADS, FEATURES, HEAD_DIM), F32),
            pltpu.VMEM((KV_HEADS, FEATURES), F32),
            dma((8,)),
            pltpu.VMEM((n_in, per, HALF, HEAD_DIM), BF16),
            pltpu.VMEM((KV_HEADS, TOK, FEATURES), BF16),
            pltpu.VMEM((KV_HEADS, AUG, FEATURES), F32),
            pltpu.VMEM((BLK, TOK), BF16),
            pltpu.VMEM((max(4 * per, KV_HEADS), HALF, TOK), F32),
            pltpu.VMEM((HEAD_DIM, FEATURES), F32),
            pltpu.VMEM((n_in, rows, FEATURES), F32),
            pltpu.VMEM((n_in, rows + 16, FEATURES), BF16),
            pltpu.VMEM((n_in, rows + 16, FEATURES), BF16),
            pltpu.VMEM((rows + 16, FEATURES), BF16),
            pltpu.VMEM((n_out, rows + 16, FEATURES), BF16),
            pltpu.VMEM((n_in, rows, FEATURES), BF16),
            pltpu.VMEM((n_in, rows, FEATURES), BF16),
            dma(()), dma((n_in,)), dma(()), dma(()),
            dma((n_out,)), dma((n_out,)), dma(()), dma(()), dma(()),
            pltpu.SemaphoreType.REGULAR,
        ],
        compiler_params=pltpu.CompilerParams(
            collective_id=0, has_side_effects=True, vmem_limit_bytes=57 << 20
        ),
    )(*args)
    return pl.pallas_call(
        functools.partial(finish, n_in // 2 == KV_HEADS),
        out_shape=jax.ShapeDtypeStruct((TOK, HEADS * HEAD_DIM), BF16),
        in_specs=[pl.BlockSpec(memory_space=pltpu.VMEM)] * 3,
        out_specs=pl.BlockSpec(memory_space=pltpu.HBM),
        scratch_shapes=[
            pltpu.VMEM((TOK, HEADS * HEAD_DIM), BF16),
            dma(()), dma(()),
        ],
        compiler_params=pltpu.CompilerParams(vmem_limit_bytes=24 << 20),
    )(rhs, lhs, done)


def solution(mesh):
    placed = (
        P(("outer", "inner"), None),
        P(("outer", "inner"), None),
        P(("outer", "inner"), None),
        P(None, ("outer", "inner")),
        P("inner", None, None),
        P(),
        P(),
        P(),
    )
    return jax.shard_map(
        functools.partial(per_device, mesh.shape["inner"], mesh.shape["outer"]),
        mesh=mesh,
        in_specs=placed,
        out_specs=P(("outer", "inner"), None),
        check_vma=False,
    )
```

```python
import functools
import jax
import jax.numpy as jnp
from jax import lax
from jax.experimental import pallas as pl
from jax.experimental.pallas import tpu as pltpu
from jax.sharding import PartitionSpec as P

HEADS = 32
KV_HEADS = 4
HEAD_DIM = 128
HALF = 64
FEATURES = 128
GROUP = 8
PAIRS = HEADS // 2
TOK = 256
BLK = 128
AUG = 144
F32 = jnp.float32
BF16 = jnp.bfloat16
MESH = pl.DeviceIdType.MESH


def dot(a, b):
    return jnp.dot(a, b, preferred_element_type=F32)


def dot_nt(a, b):
    return lax.dot_general(a, b, (((1,), (1,)), ((), ())), preferred_element_type=F32)


def features_t(u, scale=1.0):
    top = jnp.max(u, axis=0, keepdims=True)
    bottom = jnp.min(u, axis=0, keepdims=True)
    pos = jnp.exp(u - top)
    neg = jnp.exp(bottom - u)
    pos = pos * (scale / jnp.sum(pos, axis=0, keepdims=True))
    neg = neg * (scale / jnp.sum(neg, axis=0, keepdims=True))
    return jnp.concatenate([pos, neg], axis=0)


def two_parts(norm, decay):
    both = jnp.concatenate([norm, decay], axis=0)
    high = both.astype(BF16).astype(F32)
    return jnp.concatenate([high, both - high], axis=0).astype(BF16)


def unpacked(ref, j, rows, mine):
    parts = ref[j, rows:].astype(F32)
    both = parts[:8] + parts[8:]
    norm, decay = both[:KV_HEADS], both[KV_HEADS:]
    lead = decay[0:1]
    for g in range(1, KV_HEADS):
        lead = jnp.where(mine == g, decay[g : g + 1], lead)
    return ref[j, 0:rows].astype(F32), norm, decay, lead


def flipped(a, k):
    out = a
    bit = 1
    while bit <= k:
        if k & bit:
            out = out + bit - 2 * bit * lax.rem(lax.div(a, bit), 2)
        bit *= 2
    return out


def kernel(
    n_in, n_out,
    q_hbm, k_hbm, v_hbm, d_hbm, qm_hbm, km_hbm, ps_hbm, pn_hbm, rhs, lhs, done,
    q_ref, k_ref, v_ref, d_ref, km_ref, ps_ref, pn_ref, load,
    maps, keyed, early, mask, scores, prefix_t, within,
    send1, recv1, send2, recv2, send3, recv3,
    map_s, map_r, s1, r1, s2, r2, s3, r3, near, ready,
):
    me = lax.axis_index("inner")
    band = lax.axis_index("outer")
    per = HEADS // n_in
    rows = KV_HEADS * HEAD_DIM // n_in

    loads = [
        pltpu.make_async_copy(source, target, load.at[i])
        for i, (source, target) in enumerate((
            (d_hbm, d_ref), (k_hbm, k_ref), (km_hbm, km_ref), (v_hbm, v_ref),
            (qm_hbm, maps.at[me]), (q_hbm, q_ref), (ps_hbm, ps_ref), (pn_hbm, pn_ref),
        ))
    ]
    for copy in loads[:5]:
        copy.start()
    barrier = pltpu.get_barrier_semaphore()
    for k in range(n_in - 1, 0, -1):
        pl.semaphore_signal(
            barrier, inc=1, device_id={"inner": flipped(me, k)}, device_id_type=MESH
        )

    def greet_later(z, carry):
        pl.semaphore_signal(barrier, inc=1, device_id={"outer": z}, device_id_type=MESH)
        return carry

    lax.fori_loop(band + 1, n_out, greet_later, 0)

    chips = n_in // 2
    chip, core = lax.div(me, 2), lax.rem(me, 2)
    sibling = chip * 2 + 1 - core

    def map_copy(c):
        return pltpu.make_async_remote_copy(
            src_ref=maps.at[me], dst_ref=maps.at[me],
            send_sem=map_s, recv_sem=map_r.at[2 * c],
            device_id={"inner": lax.rem(chip + c, chips) * 2 + core}, device_id_type=MESH,
        )

    def map_pass(c):
        source = lax.rem(chip - c + chips, chips) * 2 + core
        return pltpu.make_async_remote_copy(
            src_ref=maps.at[source], dst_ref=maps.at[source],
            send_sem=map_s, recv_sem=map_r.at[2 * c + 1],
            device_id={"inner": sibling}, device_id_type=MESH,
        )

    def copy1(k):
        peer = flipped(me, k)
        return pltpu.make_async_remote_copy(
            src_ref=send1.at[peer], dst_ref=recv1.at[me],
            send_sem=s1, recv_sem=r1,
            device_id={"inner": peer}, device_id_type=MESH,
        )

    def copy2(source, target):
        return pltpu.make_async_remote_copy(
            src_ref=send2, dst_ref=recv2.at[source],
            send_sem=s2.at[target], recv_sem=r2.at[source],
            device_id={"outer": target}, device_id_type=MESH,
        )

    def copy3(k):
        peer = flipped(me, k)
        return pltpu.make_async_remote_copy(
            src_ref=send3.at[peer], dst_ref=recv3.at[me],
            send_sem=s3, recv_sem=near if k == 1 else r3,
            device_id={"inner": peer}, device_id_type=MESH,
        )

    others = pl.ds(0, n_in - 1)

    def all1():
        return pltpu.make_async_remote_copy(
            src_ref=send1.at[others], dst_ref=recv1.at[others], send_sem=s1, recv_sem=r1,
            device_id={"inner": sibling}, device_id_type=MESH,
        )

    def all3():
        return pltpu.make_async_remote_copy(
            src_ref=send3.at[others], dst_ref=recv3.at[others], send_sem=s3, recv_sem=r3,
            device_id={"inner": sibling}, device_id_type=MESH,
        )

    def far3():
        return pltpu.make_async_remote_copy(
            src_ref=send3.at[pl.ds(0, n_in - 2)], dst_ref=recv3.at[pl.ds(0, n_in - 2)],
            send_sem=s3, recv_sem=r3, device_id={"inner": sibling}, device_id_type=MESH,
        )

    def all_maps():
        return pltpu.make_async_remote_copy(
            src_ref=maps.at[others], dst_ref=maps.at[others], send_sem=map_s, recv_sem=map_r.at[0],
            device_id={"inner": sibling}, device_id_type=MESH,
        )

    r = lax.broadcasted_iota(jnp.int32, (BLK, BLK), 0)
    c = lax.broadcasted_iota(jnp.int32, (BLK, BLK), 1)
    upper = jnp.where(r <= c, 1.0, 0.0).astype(BF16)
    mask[:, 0:BLK] = upper
    mask[:, BLK:] = upper
    pad_row = lax.broadcasted_iota(jnp.int32, (AUG - HEAD_DIM, BLK), 0)
    ones_pad = jnp.where(pad_row == 0, 1.0, 0.0).astype(BF16)
    for g in range(KV_HEADS):
        for half in range(2):
            lhs[g, half, HEAD_DIM:, 0:BLK] = ones_pad

    for i in range(3):
        loads[i].wait()
    logs = jnp.log(d_ref[...])
    split = []
    rest = jnp.concatenate([logs[:, :BLK], logs[:, BLK:]], axis=0)
    for _ in range(3):
        part = rest.astype(BF16).astype(F32)
        split.append(part)
        rest = rest - part
    split.append(jnp.zeros_like(rest))
    summed = dot(jnp.concatenate(split, axis=0).astype(BF16), upper)
    for g in range(KV_HEADS):
        scores[g] = dot_nt(km_ref[g], k_ref[:, g * HEAD_DIM : (g + 1) * HEAD_DIM])
    local = summed[0:8] + summed[8:16] + summed[16:24]
    late = local[KV_HEADS:, BLK - 1 :]
    whole = local[:KV_HEADS, BLK - 1 :] + late
    to_end = jnp.exp(jnp.concatenate([whole, late], axis=0) - local)
    closing = jnp.broadcast_to(jnp.exp(whole), (KV_HEADS, FEATURES))
    loads[3].wait()
    for copy in loads[5:]:
        copy.start()
    for g in range(KV_HEADS):
        vt = v_ref[:, g * HEAD_DIM : (g + 1) * HEAD_DIM].T
        for half in range(2):
            lhs[g, half, 0:HEAD_DIM, 0:BLK] = vt[:, half * BLK : (half + 1) * BLK]
    for g in range(KV_HEADS):
        scale = jnp.concatenate([to_end[g : g + 1], to_end[KV_HEADS + g : KV_HEADS + g + 1]], axis=1)
        keyed[g] = features_t(scores[g], scale).astype(BF16).T
    norms = []
    for g in range(KV_HEADS):
        left = jnp.concatenate([lhs[g, 0, :, 0:BLK], lhs[g, 1, :, 0:BLK]], axis=1)
        state = dot(left, keyed[g])
        norms.append(state[HEAD_DIM : HEAD_DIM + 1])
        for part in range(HEAD_DIM // rows):
            send1[g * (HEAD_DIM // rows) + part, 0:rows] = (
                state[part * rows : (part + 1) * rows].astype(BF16)
            )
    small = two_parts(jnp.concatenate(norms, axis=0), closing)
    for j in range(n_in):
        send1[j, rows:] = small
    loads[4].wait()
    pl.semaphore_wait(barrier, n_in - 1 + band)
    for k in range(n_in - 1, 0, -1):
        copy1(k).start()

    def tell_earlier(z, carry):
        pl.semaphore_signal(ready.at[band], inc=1, device_id={"outer": z}, device_id_type=MESH)
        return carry

    lax.fori_loop(0, band, tell_earlier, 0)

    @pl.when(band == 0)
    def _():
        for c in range(1, chips):
            map_copy(c).start()

    map_pass(0).start()
    recv1[me] = send1[me]
    for g in range(KV_HEADS):
        early[g] = dot(lhs[g, 0, :, 0:BLK], keyed[g, 0:BLK])
    for i in range(5, 8):
        loads[i].wait()
    mine = lax.div(me * rows, HEAD_DIM)
    prefix_t[...] = ps_ref[mine].T

    def run_pairs(pairs):
        def project(n):
            pair, places = pairs[n]
            for e in range(2):
                h = pair * 2 + e
                q = q_ref[:, pl.ds(pl.multiple_of(h * HEAD_DIM, HEAD_DIM), HEAD_DIM)]
                source, i = places[e]
                scores[2 * n + e] = dot_nt(maps[source, i], q)

        def soften(n):
            pair = pairs[n][0]
            for e in range(2):
                feat = features_t(scores[2 * n + e]).astype(BF16)
                at = slice(e * BLK, (e + 1) * BLK)
                rhs[pair, 0, BLK:, at] = feat[:, :BLK]
                rhs[pair, 1, BLK:, at] = feat[:, BLK:]

        def weigh(n):
            pair = pairs[n][0]
            g = lax.div(pair * 2, GROUP)
            for half in range(2):
                keys = keyed[g, half * BLK : (half + 1) * BLK]
                weights = dot(keys, rhs[pair, half, BLK:])
                rhs[pair, half, 0:BLK] = weights.astype(BF16) * mask[...]

        count = len(pairs)
        project(0)
        for n in range(count + 1):
            if n + 1 < count:
                project(n + 1)
            if n < count:
                soften(n)
            if n > 0:
                weigh(n - 1)

    def heads_of(place):
        run_pairs([
            (
                place * per + n,
                [(place * 2 + m // per, m % per) for m in (2 * n, 2 * n + 1)],
            )
            for n in range(per)
        ])

    def heads_from(sources):
        run_pairs([
            (source * (per // 2) + n, [(source, 2 * n), (source, 2 * n + 1)])
            for source in sources
            for n in range(per // 2)
        ])

    def heads_later(c, carry):
        map_pass(c).wait_recv()
        heads_of(lax.rem(chip - c + chips, chips))
        return carry

    def pass_on(c, carry):
        map_copy(c).wait_recv()
        map_pass(c).start()
        return carry

    map_pass(0).wait_recv()

    @pl.when(band > 0)
    def _():
        for c in range(1, chips):
            map_copy(c).start()

    heads_of(chip)

    all1().wait_recv()
    total = jnp.zeros((rows, FEATURES), F32)
    total_norm = jnp.zeros((KV_HEADS, FEATURES), F32)
    total_decay = jnp.ones((KV_HEADS, FEATURES), F32)
    total_lead = jnp.ones((1, FEATURES), F32)
    leads = []
    my_within = total_norm
    my_decay = total_decay
    for j in range(n_in):
        block, block_norm, decay, lead = unpacked(recv1, j, rows, mine)
        total, total_norm = lead * total, decay * total_norm
        total_lead, total_decay = lead * total_lead, decay * total_decay
        within[j] = total
        leads.append(total_lead)
        my_within = jnp.where(j == me, total_norm, my_within)
        my_decay = jnp.where(j == me, total_decay, my_decay)
        total, total_norm = total + block, total_norm + block_norm
    send2[0:rows] = total.astype(BF16)
    send2[rows:] = two_parts(total_norm, total_decay)

    def send_later(z, carry):
        pl.semaphore_wait(ready.at[z], 1)
        copy2(band, z).start()
        return carry

    lax.fori_loop(band + 1, n_out, send_later, 0)

    def send_states(state):
        for j in range(n_in):
            send3[j] = (leads[j] * state + within[j]).astype(BF16)
        for k in range(n_in - 1, 0, -1):
            copy3(k).start()
        recv3[me] = send3[me]

    my_prefix = pl.ds(pl.multiple_of(lax.rem(me * rows, HEAD_DIM), rows), rows)

    @pl.when(band == 0)
    def _():
        send_states(prefix_t[my_prefix])

    lax.fori_loop(1, chips, pass_on, 0)

    def arrived(z, carry):
        copy2(z, z).wait_recv()
        return carry

    lax.fori_loop(0, band, arrived, 0)
    state = prefix_t[my_prefix]
    norm = pn_ref[...]
    for z in range(n_out - 1):
        before = z < band
        block, block_norm, decay, lead = unpacked(recv2, z, rows, mine)
        state = jnp.where(before, lead * state + block, state)
        norm = jnp.where(before, decay * norm + block_norm, norm)

    @pl.when(band > 0)
    def _():
        send_states(state)

    my_norm = my_decay * norm + my_within

    mid_norm = my_norm + jnp.concatenate(
        [early[g, HEAD_DIM : HEAD_DIM + 1] for g in range(KV_HEADS)], axis=0
    )
    pick = lax.broadcasted_iota(jnp.int32, (AUG - HEAD_DIM, FEATURES), 0)
    for half, entry in enumerate((my_norm, mid_norm)):
        high = entry.astype(BF16).astype(F32)
        low = entry - high
        for g in range(KV_HEADS):
            lhs[g, half, HEAD_DIM:, BLK:] = jnp.where(
                pick == 0, high[g : g + 1], jnp.where(pick == 1, low[g : g + 1], 0.0)
            ).astype(BF16)
    def finish_own():
        copy3(1).wait_recv()
        if chips == KV_HEADS:
            for part in range(2):
                at = slice(part * rows, (part + 1) * rows)
                entry = recv3[chip * 2 + part]
                lhs[chip, 0, at, BLK:] = entry
                lhs[chip, 1, at, BLK:] = (entry.astype(F32) + early[chip, at]).astype(BF16)
            for i in range(GROUP // 2):
                for half in range(2):
                    attend(
                        lhs[chip, half], rhs[chip * (GROUP // 2) + i, half],
                        done, half, i * 2 * HEAD_DIM,
                    )

    def heads_by_device():
        places = [lax.rem(chip - c + chips, chips) for c in range(1, chips)]
        heads_from([place * 2 + core for place in places])
        for c in range(1, chips):
            map_pass(c).wait_recv()
        heads_from([place * 2 + 1 - core for place in places])

    @pl.when(band == 0)
    def _():
        finish_own()
        lax.fori_loop(1, chips, heads_later, 0)

    @pl.when(band > 0)
    def _():
        if per % 2 == 0 and chips <= 4:
            heads_by_device()
        else:
            lax.fori_loop(1, chips, heads_later, 0)
        finish_own()

    far3().wait_recv()
    for j in range(n_in):
        g, at = divmod(j * rows, HEAD_DIM)
        entry = recv3[j]
        lhs[g, 0, at : at + rows, BLK:] = entry
        lhs[g, 1, at : at + rows, BLK:] = (
            entry.astype(F32) + early[g, at : at + rows]
        ).astype(BF16)

    all1().wait_send()
    all3().wait_send()
    all_maps().wait_send()

    def sent(z, carry):
        copy2(band, z).wait_send()
        return carry

    lax.fori_loop(band + 1, n_out, sent, 0)


def attend(left, right, out_ref, half, column):
    full = dot(left, right)
    den = full[HEAD_DIM : HEAD_DIM + 1] + full[HEAD_DIM + 1 : HEAD_DIM + 2]
    out = (full[:HEAD_DIM] * (1.0 / den)).astype(BF16)
    for i in range(2):
        at = column + i * HEAD_DIM
        out_ref[half * BLK : (half + 1) * BLK, at : at + HEAD_DIM] = (
            out[:, i * BLK : (i + 1) * BLK].T
        )


def finish(ready_made, rhs_ref, lhs_ref, done_ref, o_hbm, o_ref, drain, drain_done):
    wide = GROUP * HEAD_DIM
    left_over = KV_HEADS
    own = 0
    if ready_made:
        left_over = KV_HEADS - 1
        own = lax.div(lax.axis_index("inner"), 2)
        early_out = pltpu.make_async_copy(
            done_ref, o_hbm.at[:, pl.ds(pl.multiple_of(own * wide, wide), wide)], drain_done
        )
        early_out.start()
    for n in range(left_over):
        g = lax.rem(own + 1 + n, KV_HEADS)
        for i in range(GROUP // 2):
            column = n * wide + i * 2 * HEAD_DIM
            for half in range(2):
                attend(lhs_ref[g, half], rhs_ref[g * (GROUP // 2) + i, half], o_ref, half, column)
            target = pl.multiple_of(g * wide + i * 2 * HEAD_DIM, 2 * HEAD_DIM)
            pltpu.make_async_copy(
                o_ref.at[:, pl.ds(column, 2 * HEAD_DIM)],
                o_hbm.at[:, pl.ds(target, 2 * HEAD_DIM)], drain,
            ).start()
    pltpu.make_async_copy(
        o_ref.at[:, pl.ds(0, left_over * wide)], o_hbm.at[:, pl.ds(0, left_over * wide)], drain
    ).wait()
    if ready_made:
        early_out.wait()


def per_device(n_in, n_out, q, k, v, d, query_map, key_map, prefix_state, prefix_norm):
    args = (
        q, k, v, d, jnp.swapaxes(query_map, 1, 2), jnp.swapaxes(key_map, 1, 2),
        prefix_state, prefix_norm,
    )
    per = HEADS // n_in
    rows = KV_HEADS * HEAD_DIM // n_in
    dma = pltpu.SemaphoreType.DMA
    rhs, lhs, done = pl.pallas_call(
        functools.partial(kernel, n_in, n_out),
        out_shape=(
            pltpu.VMEM((PAIRS, 2, TOK, TOK), BF16),
            pltpu.VMEM((KV_HEADS, 2, AUG, TOK), BF16),
            pltpu.VMEM((TOK, GROUP * HEAD_DIM), BF16),
        ),
        in_specs=[pl.BlockSpec(memory_space=pltpu.HBM)] * 8,
        out_specs=(pl.BlockSpec(memory_space=pltpu.VMEM),) * 3,
        scratch_shapes=[
            pltpu.VMEM((TOK, HEADS * HEAD_DIM), BF16),
            pltpu.VMEM((TOK, KV_HEADS * HEAD_DIM), BF16),
            pltpu.VMEM((TOK, KV_HEADS * HEAD_DIM), BF16),
            pltpu.VMEM((KV_HEADS, TOK), F32),
            pltpu.VMEM((KV_HEADS, HALF, HEAD_DIM), BF16),
            pltpu.VMEM((KV_HEADS, FEATURES, HEAD_DIM), F32),
            pltpu.VMEM((KV_HEADS, FEATURES), F32),
            dma((8,)),
            pltpu.VMEM((n_in, per, HALF, HEAD_DIM), BF16),
            pltpu.VMEM((KV_HEADS, TOK, FEATURES), BF16),
            pltpu.VMEM((KV_HEADS, AUG, FEATURES), F32),
            pltpu.VMEM((BLK, TOK), BF16),
            pltpu.VMEM((max(4 * per, KV_HEADS), HALF, TOK), F32),
            pltpu.VMEM((HEAD_DIM, FEATURES), F32),
            pltpu.VMEM((n_in, rows, FEATURES), F32),
            pltpu.VMEM((n_in, rows + 16, FEATURES), BF16),
            pltpu.VMEM((n_in, rows + 16, FEATURES), BF16),
            pltpu.VMEM((rows + 16, FEATURES), BF16),
            pltpu.VMEM((n_out, rows + 16, FEATURES), BF16),
            pltpu.VMEM((n_in, rows, FEATURES), BF16),
            pltpu.VMEM((n_in, rows, FEATURES), BF16),
            dma(()), dma((n_in,)), dma(()), dma(()),
            dma((n_out,)), dma((n_out,)), dma(()), dma(()), dma(()),
            pltpu.SemaphoreType.REGULAR((n_out,)),
        ],
        compiler_params=pltpu.CompilerParams(
            collective_id=0, has_side_effects=True, vmem_limit_bytes=57 << 20
        ),
    )(*args)
    return pl.pallas_call(
        functools.partial(finish, n_in // 2 == KV_HEADS),
        out_shape=jax.ShapeDtypeStruct((TOK, HEADS * HEAD_DIM), BF16),
        in_specs=[pl.BlockSpec(memory_space=pltpu.VMEM)] * 3,
        out_specs=pl.BlockSpec(memory_space=pltpu.HBM),
        scratch_shapes=[
            pltpu.VMEM((TOK, HEADS * HEAD_DIM), BF16),
            dma(()), dma(()),
        ],
        compiler_params=pltpu.CompilerParams(vmem_limit_bytes=24 << 20),
    )(rhs, lhs, done)


def solution(mesh):
    placed = (
        P(("outer", "inner"), None),
        P(("outer", "inner"), None),
        P(("outer", "inner"), None),
        P(None, ("outer", "inner")),
        P("inner", None, None),
        P(),
        P(),
        P(),
    )
    return jax.shard_map(
        functools.partial(per_device, mesh.shape["inner"], mesh.shape["outer"]),
        mesh=mesh,
        in_specs=placed,
        out_specs=P(("outer", "inner"), None),
        check_vma=False,
    )
```

```python
import functools
import jax
import jax.numpy as jnp
from jax import lax
from jax.experimental import pallas as pl
from jax.experimental.pallas import tpu as pltpu
from jax.sharding import PartitionSpec as P

HEADS = 32
KV_HEADS = 4
HEAD_DIM = 128
HALF = 64
FEATURES = 128
GROUP = 8
PAIRS = HEADS // 2
TOK = 256
BLK = 128
AUG = 144
F32 = jnp.float32
BF16 = jnp.bfloat16
MESH = pl.DeviceIdType.MESH


def dot(a, b):
    return jnp.dot(a, b, preferred_element_type=F32)


def dot_nt(a, b):
    return lax.dot_general(a, b, (((1,), (1,)), ((), ())), preferred_element_type=F32)


def features_t(u, scale=1.0):
    top = jnp.max(u, axis=0, keepdims=True)
    bottom = jnp.min(u, axis=0, keepdims=True)
    pos = jnp.exp(u - top)
    neg = jnp.exp(bottom - u)
    pos = pos * (scale / jnp.sum(pos, axis=0, keepdims=True))
    neg = neg * (scale / jnp.sum(neg, axis=0, keepdims=True))
    return jnp.concatenate([pos, neg], axis=0)


def two_parts(norm, decay):
    both = jnp.concatenate([norm, decay], axis=0)
    high = both.astype(BF16).astype(F32)
    return jnp.concatenate([high, both - high], axis=0).astype(BF16)


def unpacked(ref, j, rows, mine):
    parts = ref[j, rows:].astype(F32)
    both = parts[:8] + parts[8:]
    norm, decay = both[:KV_HEADS], both[KV_HEADS:]
    lead = decay[0:1]
    for g in range(1, KV_HEADS):
        lead = jnp.where(mine == g, decay[g : g + 1], lead)
    return ref[j, 0:rows].astype(F32), norm, decay, lead


def flipped(a, k):
    out = a
    bit = 1
    while bit <= k:
        if k & bit:
            out = out + bit - 2 * bit * lax.rem(lax.div(a, bit), 2)
        bit *= 2
    return out


def kernel(
    n_in, n_out,
    q_hbm, k_hbm, v_hbm, d_hbm, qm_hbm, km_hbm, ps_hbm, pn_hbm, rhs, lhs, done,
    q_ref, k_ref, v_ref, d_ref, km_ref, ps_ref, pn_ref, load,
    maps, keyed, early, mask, scores, prefix_t, within,
    send1, recv1, send2, recv2, send3, recv3,
    map_s, map_r, s1, r1, s2, r2, s3, r3, near, ready,
):
    me = lax.axis_index("inner")
    band = lax.axis_index("outer")
    per = HEADS // n_in
    rows = KV_HEADS * HEAD_DIM // n_in

    loads = [
        pltpu.make_async_copy(source, target, load.at[i])
        for i, (source, target) in enumerate((
            (d_hbm, d_ref), (k_hbm, k_ref), (km_hbm, km_ref), (v_hbm, v_ref),
            (qm_hbm, maps.at[me]), (q_hbm, q_ref), (ps_hbm, ps_ref), (pn_hbm, pn_ref),
        ))
    ]
    for copy in loads[:5]:
        copy.start()
    barrier = pltpu.get_barrier_semaphore()
    for k in range(n_in - 1, 0, -1):
        pl.semaphore_signal(
            barrier, inc=1, device_id={"inner": flipped(me, k)}, device_id_type=MESH
        )

    def greet_later(z, carry):
        pl.semaphore_signal(barrier, inc=1, device_id={"outer": z}, device_id_type=MESH)
        return carry

    lax.fori_loop(band + 1, n_out, greet_later, 0)

    chips = n_in // 2
    chip, core = lax.div(me, 2), lax.rem(me, 2)
    sibling = chip * 2 + 1 - core

    def map_copy(c):
        return pltpu.make_async_remote_copy(
            src_ref=maps.at[me], dst_ref=maps.at[me],
            send_sem=map_s, recv_sem=map_r.at[2 * c],
            device_id={"inner": lax.rem(chip + c, chips) * 2 + core}, device_id_type=MESH,
        )

    def send_maps():
        for target in range(chips):
            @pl.when(target != chip)
            def _():
                map_copy(lax.rem(target - chip + chips, chips)).start()

    def map_pass(c):
        source = lax.rem(chip - c + chips, chips) * 2 + core
        return pltpu.make_async_remote_copy(
            src_ref=maps.at[source], dst_ref=maps.at[source],
            send_sem=map_s, recv_sem=map_r.at[2 * c + 1],
            device_id={"inner": sibling}, device_id_type=MESH,
        )

    def copy1(k):
        peer = flipped(me, k)
        return pltpu.make_async_remote_copy(
            src_ref=send1.at[peer], dst_ref=recv1.at[me],
            send_sem=s1, recv_sem=r1,
            device_id={"inner": peer}, device_id_type=MESH,
        )

    def copy2(source, target):
        return pltpu.make_async_remote_copy(
            src_ref=send2, dst_ref=recv2.at[source],
            send_sem=s2.at[target], recv_sem=r2.at[source],
            device_id={"outer": target}, device_id_type=MESH,
        )

    def copy3(k):
        peer = flipped(me, k)
        return pltpu.make_async_remote_copy(
            src_ref=send3.at[peer], dst_ref=recv3.at[me],
            send_sem=s3, recv_sem=near if k == 1 else r3,
            device_id={"inner": peer}, device_id_type=MESH,
        )

    others = pl.ds(0, n_in - 1)

    def all1():
        return pltpu.make_async_remote_copy(
            src_ref=send1.at[others], dst_ref=recv1.at[others], send_sem=s1, recv_sem=r1,
            device_id={"inner": sibling}, device_id_type=MESH,
        )

    def all3():
        return pltpu.make_async_remote_copy(
            src_ref=send3.at[others], dst_ref=recv3.at[others], send_sem=s3, recv_sem=r3,
            device_id={"inner": sibling}, device_id_type=MESH,
        )

    def far3():
        return pltpu.make_async_remote_copy(
            src_ref=send3.at[pl.ds(0, n_in - 2)], dst_ref=recv3.at[pl.ds(0, n_in - 2)],
            send_sem=s3, recv_sem=r3, device_id={"inner": sibling}, device_id_type=MESH,
        )

    def all_maps():
        return pltpu.make_async_remote_copy(
            src_ref=maps.at[others], dst_ref=maps.at[others], send_sem=map_s, recv_sem=map_r.at[0],
            device_id={"inner": sibling}, device_id_type=MESH,
        )

    r = lax.broadcasted_iota(jnp.int32, (BLK, BLK), 0)
    c = lax.broadcasted_iota(jnp.int32, (BLK, BLK), 1)
    upper = jnp.where(r <= c, 1.0, 0.0).astype(BF16)
    mask[:, 0:BLK] = upper
    mask[:, BLK:] = upper
    pad_row = lax.broadcasted_iota(jnp.int32, (AUG - HEAD_DIM, BLK), 0)
    ones_pad = jnp.where(pad_row == 0, 1.0, 0.0).astype(BF16)
    for g in range(KV_HEADS):
        for half in range(2):
            lhs[g, half, HEAD_DIM:, 0:BLK] = ones_pad

    for i in range(3):
        loads[i].wait()
    logs = jnp.log(d_ref[...])
    split = []
    rest = jnp.concatenate([logs[:, :BLK], logs[:, BLK:]], axis=0)
    for _ in range(3):
        part = rest.astype(BF16).astype(F32)
        split.append(part)
        rest = rest - part
    split.append(jnp.zeros_like(rest))
    summed = dot(jnp.concatenate(split, axis=0).astype(BF16), upper)
    for g in range(KV_HEADS):
        scores[g] = dot_nt(km_ref[g], k_ref[:, g * HEAD_DIM : (g + 1) * HEAD_DIM])
    local = summed[0:8] + summed[8:16] + summed[16:24]
    late = local[KV_HEADS:, BLK - 1 :]
    whole = local[:KV_HEADS, BLK - 1 :] + late
    to_end = jnp.exp(jnp.concatenate([whole, late], axis=0) - local)
    closing = jnp.broadcast_to(jnp.exp(whole), (KV_HEADS, FEATURES))
    loads[3].wait()
    for copy in loads[5:]:
        copy.start()
    for g in range(KV_HEADS):
        vt = v_ref[:, g * HEAD_DIM : (g + 1) * HEAD_DIM].T
        for half in range(2):
            lhs[g, half, 0:HEAD_DIM, 0:BLK] = vt[:, half * BLK : (half + 1) * BLK]
    for g in range(KV_HEADS):
        scale = jnp.concatenate([to_end[g : g + 1], to_end[KV_HEADS + g : KV_HEADS + g + 1]], axis=1)
        keyed[g] = features_t(scores[g], scale).astype(BF16).T
    norms = []
    for g in range(KV_HEADS):
        left = jnp.concatenate([lhs[g, 0, :, 0:BLK], lhs[g, 1, :, 0:BLK]], axis=1)
        state = dot(left, keyed[g])
        norms.append(state[HEAD_DIM : HEAD_DIM + 1])
        for part in range(HEAD_DIM // rows):
            send1[g * (HEAD_DIM // rows) + part, 0:rows] = (
                state[part * rows : (part + 1) * rows].astype(BF16)
            )
    small = two_parts(jnp.concatenate(norms, axis=0), closing)
    for j in range(n_in):
        send1[j, rows:] = small
    loads[4].wait()
    pl.semaphore_wait(barrier, n_in - 1 + band)
    for k in range(n_in - 1, 0, -1):
        copy1(k).start()

    def tell_earlier(z, carry):
        pl.semaphore_signal(ready, inc=1, device_id={"outer": z}, device_id_type=MESH)
        return carry

    lax.fori_loop(0, band, tell_earlier, 0)

    @pl.when(band == 0)
    def _():
        send_maps()

    map_pass(0).start()
    recv1[me] = send1[me]
    for g in range(KV_HEADS):
        early[g] = dot(lhs[g, 0, :, 0:BLK], keyed[g, 0:BLK])
    for i in range(5, 8):
        loads[i].wait()
    mine = lax.div(me * rows, HEAD_DIM)
    prefix_t[...] = ps_ref[mine].T

    def run_pairs(pairs):
        def project(n):
            pair, places = pairs[n]
            for e in range(2):
                h = pair * 2 + e
                q = q_ref[:, pl.ds(pl.multiple_of(h * HEAD_DIM, HEAD_DIM), HEAD_DIM)]
                source, i = places[e]
                scores[2 * n + e] = dot_nt(maps[source, i], q)

        def soften(n):
            pair = pairs[n][0]
            for e in range(2):
                feat = features_t(scores[2 * n + e]).astype(BF16)
                at = slice(e * BLK, (e + 1) * BLK)
                rhs[pair, 0, BLK:, at] = feat[:, :BLK]
                rhs[pair, 1, BLK:, at] = feat[:, BLK:]

        def weigh(n):
            pair = pairs[n][0]
            g = lax.div(pair * 2, GROUP)
            for half in range(2):
                keys = keyed[g, half * BLK : (half + 1) * BLK]
                weights = dot(keys, rhs[pair, half, BLK:])
                rhs[pair, half, 0:BLK] = weights.astype(BF16) * mask[...]

        count = len(pairs)
        project(0)
        for n in range(count + 1):
            if n + 1 < count:
                project(n + 1)
            if n < count:
                soften(n)
            if n > 0:
                weigh(n - 1)

    def heads_of(place):
        run_pairs([
            (
                place * per + n,
                [(place * 2 + m // per, m % per) for m in (2 * n, 2 * n + 1)],
            )
            for n in range(per)
        ])

    def heads_from(sources):
        run_pairs([
            (source * (per // 2) + n, [(source, 2 * n), (source, 2 * n + 1)])
            for source in sources
            for n in range(per // 2)
        ])

    def heads_later(c, carry):
        map_pass(c).wait_recv()
        heads_of(lax.rem(chip - c + chips, chips))
        return carry

    def pass_on(c, carry):
        map_copy(c).wait_recv()
        map_pass(c).start()
        return carry

    map_pass(0).wait_recv()
    heads_of(chip)

    @pl.when(band > 0)
    def _():
        send_maps()


    all1().wait_recv()
    total = jnp.zeros((rows, FEATURES), F32)
    total_norm = jnp.zeros((KV_HEADS, FEATURES), F32)
    total_decay = jnp.ones((KV_HEADS, FEATURES), F32)
    total_lead = jnp.ones((1, FEATURES), F32)
    leads = []
    my_within = total_norm
    my_decay = total_decay
    for j in range(n_in):
        block, block_norm, decay, lead = unpacked(recv1, j, rows, mine)
        total, total_norm = lead * total, decay * total_norm
        total_lead, total_decay = lead * total_lead, decay * total_decay
        within[j] = total
        leads.append(total_lead)
        my_within = jnp.where(j == me, total_norm, my_within)
        my_decay = jnp.where(j == me, total_decay, my_decay)
        total, total_norm = total + block, total_norm + block_norm
    send2[0:rows] = total.astype(BF16)
    send2[rows:] = two_parts(total_norm, total_decay)

    @pl.when(band < n_out - 1)
    def _():
        pl.semaphore_wait(ready, n_out - 1 - band)

    def send_later(z, carry):
        copy2(band, z).start()
        return carry

    lax.fori_loop(band + 1, n_out, send_later, 0)

    def send_states(state):
        for j in range(n_in):
            send3[j] = (leads[j] * state + within[j]).astype(BF16)
        recv3[me] = send3[me]

    my_prefix = pl.ds(pl.multiple_of(lax.rem(me * rows, HEAD_DIM), rows), rows)

    @pl.when(band == 0)
    def _():
        send_states(prefix_t[my_prefix])
        for k in range(n_in - 1, 1, -1):
            @pl.when(flipped(me, k) < 2)
            def _():
                copy3(k).start()
        copy3(1).start()

    lax.fori_loop(1, chips, pass_on, 0)

    @pl.when(band == 0)
    def _():
        for k in range(n_in - 1, 1, -1):
            @pl.when(flipped(me, k) >= 2)
            def _():
                copy3(k).start()


    def arrived(z, carry):
        copy2(z, z).wait_recv()
        return carry

    lax.fori_loop(0, band, arrived, 0)
    state = prefix_t[my_prefix]
    norm = pn_ref[...]
    for z in range(n_out - 1):
        before = z < band
        block, block_norm, decay, lead = unpacked(recv2, z, rows, mine)
        state = jnp.where(before, lead * state + block, state)
        norm = jnp.where(before, decay * norm + block_norm, norm)

    @pl.when(band > 0)
    def _():
        send_states(state)
        for k in range(n_in - 1, 0, -1):
            copy3(k).start()

    my_norm = my_decay * norm + my_within

    mid_norm = my_norm + jnp.concatenate(
        [early[g, HEAD_DIM : HEAD_DIM + 1] for g in range(KV_HEADS)], axis=0
    )
    pick = lax.broadcasted_iota(jnp.int32, (AUG - HEAD_DIM, FEATURES), 0)
    for half, entry in enumerate((my_norm, mid_norm)):
        high = entry.astype(BF16).astype(F32)
        low = entry - high
        for g in range(KV_HEADS):
            lhs[g, half, HEAD_DIM:, BLK:] = jnp.where(
                pick == 0, high[g : g + 1], jnp.where(pick == 1, low[g : g + 1], 0.0)
            ).astype(BF16)
    def finish_own():
        copy3(1).wait_recv()
        if chips == KV_HEADS:
            for part in range(2):
                at = slice(part * rows, (part + 1) * rows)
                entry = recv3[chip * 2 + part]
                lhs[chip, 0, at, BLK:] = entry
                lhs[chip, 1, at, BLK:] = (entry.astype(F32) + early[chip, at]).astype(BF16)
            for i in range(GROUP // 2):
                for half in range(2):
                    attend(
                        lhs[chip, half], rhs[chip * (GROUP // 2) + i, half],
                        done, half, i * 2 * HEAD_DIM,
                    )

    def heads_by_device():
        places = [lax.rem(chip - c + chips, chips) for c in range(1, chips)]
        heads_from([place * 2 + core for place in places])
        for c in range(1, chips):
            map_pass(c).wait_recv()
        heads_from([place * 2 + 1 - core for place in places])

    @pl.when(band == 0)
    def _():
        finish_own()
        lax.fori_loop(1, chips, heads_later, 0)

    @pl.when(band > 0)
    def _():
        if per % 2 == 0 and chips <= 4:
            heads_by_device()
        else:
            lax.fori_loop(1, chips, heads_later, 0)
        finish_own()

    far3().wait_recv()
    for j in range(n_in):
        g, at = divmod(j * rows, HEAD_DIM)
        entry = recv3[j]
        lhs[g, 0, at : at + rows, BLK:] = entry
        lhs[g, 1, at : at + rows, BLK:] = (
            entry.astype(F32) + early[g, at : at + rows]
        ).astype(BF16)

    all1().wait_send()
    all3().wait_send()
    all_maps().wait_send()

    def sent(z, carry):
        copy2(band, z).wait_send()
        return carry

    lax.fori_loop(band + 1, n_out, sent, 0)


def attend(left, right, out_ref, half, column):
    full = dot(left, right)
    den = full[HEAD_DIM : HEAD_DIM + 1] + full[HEAD_DIM + 1 : HEAD_DIM + 2]
    out = (full[:HEAD_DIM] * (1.0 / den)).astype(BF16)
    for i in range(2):
        at = column + i * HEAD_DIM
        out_ref[half * BLK : (half + 1) * BLK, at : at + HEAD_DIM] = (
            out[:, i * BLK : (i + 1) * BLK].T
        )


def finish(ready_made, rhs_ref, lhs_ref, done_ref, o_hbm, o_ref, drain, drain_done):
    wide = GROUP * HEAD_DIM
    left_over = KV_HEADS
    own = 0
    if ready_made:
        left_over = KV_HEADS - 1
        own = lax.div(lax.axis_index("inner"), 2)
        early_out = pltpu.make_async_copy(
            done_ref, o_hbm.at[:, pl.ds(pl.multiple_of(own * wide, wide), wide)], drain_done
        )
        early_out.start()
    for n in range(left_over):
        g = lax.rem(own + 1 + n, KV_HEADS)
        for i in range(GROUP // 2):
            column = n * wide + i * 2 * HEAD_DIM
            for half in range(2):
                attend(lhs_ref[g, half], rhs_ref[g * (GROUP // 2) + i, half], o_ref, half, column)
            target = pl.multiple_of(g * wide + i * 2 * HEAD_DIM, 2 * HEAD_DIM)
            pltpu.make_async_copy(
                o_ref.at[:, pl.ds(column, 2 * HEAD_DIM)],
                o_hbm.at[:, pl.ds(target, 2 * HEAD_DIM)], drain,
            ).start()
    pltpu.make_async_copy(
        o_ref.at[:, pl.ds(0, left_over * wide)], o_hbm.at[:, pl.ds(0, left_over * wide)], drain
    ).wait()
    if ready_made:
        early_out.wait()


def per_device(n_in, n_out, q, k, v, d, query_map, key_map, prefix_state, prefix_norm):
    args = (
        q, k, v, d, jnp.swapaxes(query_map, 1, 2), jnp.swapaxes(key_map, 1, 2),
        prefix_state, prefix_norm,
    )
    per = HEADS // n_in
    rows = KV_HEADS * HEAD_DIM // n_in
    dma = pltpu.SemaphoreType.DMA
    rhs, lhs, done = pl.pallas_call(
        functools.partial(kernel, n_in, n_out),
        out_shape=(
            pltpu.VMEM((PAIRS, 2, TOK, TOK), BF16),
            pltpu.VMEM((KV_HEADS, 2, AUG, TOK), BF16),
            pltpu.VMEM((TOK, GROUP * HEAD_DIM), BF16),
        ),
        in_specs=[pl.BlockSpec(memory_space=pltpu.HBM)] * 8,
        out_specs=(pl.BlockSpec(memory_space=pltpu.VMEM),) * 3,
        scratch_shapes=[
            pltpu.VMEM((TOK, HEADS * HEAD_DIM), BF16),
            pltpu.VMEM((TOK, KV_HEADS * HEAD_DIM), BF16),
            pltpu.VMEM((TOK, KV_HEADS * HEAD_DIM), BF16),
            pltpu.VMEM((KV_HEADS, TOK), F32),
            pltpu.VMEM((KV_HEADS, HALF, HEAD_DIM), BF16),
            pltpu.VMEM((KV_HEADS, FEATURES, HEAD_DIM), F32),
            pltpu.VMEM((KV_HEADS, FEATURES), F32),
            dma((8,)),
            pltpu.VMEM((n_in, per, HALF, HEAD_DIM), BF16),
            pltpu.VMEM((KV_HEADS, TOK, FEATURES), BF16),
            pltpu.VMEM((KV_HEADS, AUG, FEATURES), F32),
            pltpu.VMEM((BLK, TOK), BF16),
            pltpu.VMEM((max(4 * per, KV_HEADS), HALF, TOK), F32),
            pltpu.VMEM((HEAD_DIM, FEATURES), F32),
            pltpu.VMEM((n_in, rows, FEATURES), F32),
            pltpu.VMEM((n_in, rows + 16, FEATURES), BF16),
            pltpu.VMEM((n_in, rows + 16, FEATURES), BF16),
            pltpu.VMEM((rows + 16, FEATURES), BF16),
            pltpu.VMEM((n_out, rows + 16, FEATURES), BF16),
            pltpu.VMEM((n_in, rows, FEATURES), BF16),
            pltpu.VMEM((n_in, rows, FEATURES), BF16),
            dma(()), dma((n_in,)), dma(()), dma(()),
            dma((n_out,)), dma((n_out,)), dma(()), dma(()), dma(()),
            pltpu.SemaphoreType.REGULAR,
        ],
        compiler_params=pltpu.CompilerParams(
            collective_id=0, has_side_effects=True, vmem_limit_bytes=57 << 20
        ),
    )(*args)
    return pl.pallas_call(
        functools.partial(finish, n_in // 2 == KV_HEADS),
        out_shape=jax.ShapeDtypeStruct((TOK, HEADS * HEAD_DIM), BF16),
        in_specs=[pl.BlockSpec(memory_space=pltpu.VMEM)] * 3,
        out_specs=pl.BlockSpec(memory_space=pltpu.HBM),
        scratch_shapes=[
            pltpu.VMEM((TOK, HEADS * HEAD_DIM), BF16),
            dma(()), dma(()),
        ],
        compiler_params=pltpu.CompilerParams(vmem_limit_bytes=24 << 20),
    )(rhs, lhs, done)


def solution(mesh):
    placed = (
        P(("outer", "inner"), None),
        P(("outer", "inner"), None),
        P(("outer", "inner"), None),
        P(None, ("outer", "inner")),
        P("inner", None, None),
        P(),
        P(),
        P(),
    )
    return jax.shard_map(
        functools.partial(per_device, mesh.shape["inner"], mesh.shape["outer"]),
        mesh=mesh,
        in_specs=placed,
        out_specs=P(("outer", "inner"), None),
        check_vma=False,
    )
```

```python
import functools
import jax
import jax.numpy as jnp
from jax import lax
from jax.experimental import pallas as pl
from jax.experimental.pallas import tpu as pltpu
from jax.sharding import PartitionSpec as P

HEADS = 32
KV_HEADS = 4
HEAD_DIM = 128
HALF = 64
FEATURES = 128
GROUP = 8
PAIRS = HEADS // 2
TOK = 256
BLK = 128
AUG = 144
F32 = jnp.float32
BF16 = jnp.bfloat16
MESH = pl.DeviceIdType.MESH


def dot(a, b):
    return jnp.dot(a, b, preferred_element_type=F32)


def dot_nt(a, b):
    return lax.dot_general(a, b, (((1,), (1,)), ((), ())), preferred_element_type=F32)


def features_t(u, scale=1.0):
    top = jnp.max(u, axis=0, keepdims=True)
    bottom = jnp.min(u, axis=0, keepdims=True)
    pos = jnp.exp(u - top)
    neg = jnp.exp(bottom - u)
    pos = pos * (scale / jnp.sum(pos, axis=0, keepdims=True))
    neg = neg * (scale / jnp.sum(neg, axis=0, keepdims=True))
    return jnp.concatenate([pos, neg], axis=0)


def two_parts(norm, decay):
    both = jnp.concatenate([norm, decay], axis=0)
    high = both.astype(BF16).astype(F32)
    return jnp.concatenate([high, both - high], axis=0).astype(BF16)


def unpacked(ref, j, rows, mine):
    parts = ref[j, rows:].astype(F32)
    both = parts[:8] + parts[8:]
    norm, decay = both[:KV_HEADS], both[KV_HEADS:]
    lead = decay[0:1]
    for g in range(1, KV_HEADS):
        lead = jnp.where(mine == g, decay[g : g + 1], lead)
    return ref[j, 0:rows].astype(F32), norm, decay, lead


def flipped(a, k):
    out = a
    bit = 1
    while bit <= k:
        if k & bit:
            out = out + bit - 2 * bit * lax.rem(lax.div(a, bit), 2)
        bit *= 2
    return out


def kernel(
    n_in, n_out,
    q_hbm, k_hbm, v_hbm, d_hbm, qm_hbm, km_hbm, ps_hbm, pn_hbm, rhs, lhs, done,
    q_ref, k_ref, v_ref, d_ref, km_ref, ps_ref, pn_ref, load,
    maps, keyed, early, mask, scores, prefix_t, within,
    send1, recv1, send2, recv2, send3, recv3,
    map_s, map_r, s1, r1, s2, r2, s3, r3, near, ready,
):
    me = lax.axis_index("inner")
    band = lax.axis_index("outer")
    per = HEADS // n_in
    rows = KV_HEADS * HEAD_DIM // n_in

    loads = [
        pltpu.make_async_copy(source, target, load.at[i])
        for i, (source, target) in enumerate((
            (d_hbm, d_ref), (k_hbm, k_ref), (km_hbm, km_ref), (v_hbm, v_ref),
            (qm_hbm, maps.at[me]), (q_hbm, q_ref), (ps_hbm, ps_ref), (pn_hbm, pn_ref),
        ))
    ]
    for i in (1, 2, 0, 3, 4):
        loads[i].start()
    barrier = pltpu.get_barrier_semaphore()
    for k in range(n_in - 1, 0, -1):
        pl.semaphore_signal(
            barrier, inc=1, device_id={"inner": flipped(me, k)}, device_id_type=MESH
        )

    def greet_later(z, carry):
        pl.semaphore_signal(barrier, inc=1, device_id={"outer": z}, device_id_type=MESH)
        return carry

    lax.fori_loop(band + 1, n_out, greet_later, 0)

    chips = n_in // 2
    chip, core = lax.div(me, 2), lax.rem(me, 2)
    sibling = chip * 2 + 1 - core

    def map_copy(c):
        return pltpu.make_async_remote_copy(
            src_ref=maps.at[me], dst_ref=maps.at[me],
            send_sem=map_s, recv_sem=map_r.at[2 * c],
            device_id={"inner": lax.rem(chip + c, chips) * 2 + core}, device_id_type=MESH,
        )

    def map_pass(c):
        source = lax.rem(chip - c + chips, chips) * 2 + core
        return pltpu.make_async_remote_copy(
            src_ref=maps.at[source], dst_ref=maps.at[source],
            send_sem=map_s, recv_sem=map_r.at[2 * c + 1],
            device_id={"inner": sibling}, device_id_type=MESH,
        )

    def copy1(k):
        peer = flipped(me, k)
        return pltpu.make_async_remote_copy(
            src_ref=send1.at[peer], dst_ref=recv1.at[me],
            send_sem=s1, recv_sem=r1,
            device_id={"inner": peer}, device_id_type=MESH,
        )

    def copy2(source, target):
        return pltpu.make_async_remote_copy(
            src_ref=send2, dst_ref=recv2.at[source],
            send_sem=s2.at[target], recv_sem=r2.at[source],
            device_id={"outer": target}, device_id_type=MESH,
        )

    def copy3(k):
        peer = flipped(me, k)
        return pltpu.make_async_remote_copy(
            src_ref=send3.at[peer], dst_ref=recv3.at[me],
            send_sem=s3, recv_sem=near if k == 1 else r3,
            device_id={"inner": peer}, device_id_type=MESH,
        )

    others = pl.ds(0, n_in - 1)

    def all1():
        return pltpu.make_async_remote_copy(
            src_ref=send1.at[others], dst_ref=recv1.at[others], send_sem=s1, recv_sem=r1,
            device_id={"inner": sibling}, device_id_type=MESH,
        )

    def all3():
        return pltpu.make_async_remote_copy(
            src_ref=send3.at[others], dst_ref=recv3.at[others], send_sem=s3, recv_sem=r3,
            device_id={"inner": sibling}, device_id_type=MESH,
        )

    def far3():
        return pltpu.make_async_remote_copy(
            src_ref=send3.at[pl.ds(0, n_in - 2)], dst_ref=recv3.at[pl.ds(0, n_in - 2)],
            send_sem=s3, recv_sem=r3, device_id={"inner": sibling}, device_id_type=MESH,
        )

    def all_maps():
        return pltpu.make_async_remote_copy(
            src_ref=maps.at[others], dst_ref=maps.at[others], send_sem=map_s, recv_sem=map_r.at[0],
            device_id={"inner": sibling}, device_id_type=MESH,
        )

    r = lax.broadcasted_iota(jnp.int32, (BLK, BLK), 0)
    c = lax.broadcasted_iota(jnp.int32, (BLK, BLK), 1)
    upper = jnp.where(r <= c, 1.0, 0.0).astype(BF16)
    mask[:, 0:BLK] = upper
    mask[:, BLK:] = upper
    pad_row = lax.broadcasted_iota(jnp.int32, (AUG - HEAD_DIM, BLK), 0)
    ones_pad = jnp.where(pad_row == 0, 1.0, 0.0).astype(BF16)
    for g in range(KV_HEADS):
        for half in range(2):
            lhs[g, half, HEAD_DIM:, 0:BLK] = ones_pad

    loads[1].wait()
    loads[2].wait()
    for g in range(KV_HEADS):
        scores[g] = dot_nt(km_ref[g], k_ref[:, g * HEAD_DIM : (g + 1) * HEAD_DIM])
    loads[0].wait()
    logs = jnp.log(d_ref[...])
    split = []
    rest = jnp.concatenate([logs[:, :BLK], logs[:, BLK:]], axis=0)
    for _ in range(3):
        part = rest.astype(BF16).astype(F32)
        split.append(part)
        rest = rest - part
    split.append(jnp.zeros_like(rest))
    summed = dot(jnp.concatenate(split, axis=0).astype(BF16), upper)
    local = summed[0:8] + summed[8:16] + summed[16:24]
    late = local[KV_HEADS:, BLK - 1 :]
    whole = local[:KV_HEADS, BLK - 1 :] + late
    to_end = jnp.exp(jnp.concatenate([whole, late], axis=0) - local)
    closing = jnp.broadcast_to(jnp.exp(whole), (KV_HEADS, FEATURES))
    loads[3].wait()
    for copy in loads[5:]:
        copy.start()
    for g in range(KV_HEADS):
        vt = v_ref[:, g * HEAD_DIM : (g + 1) * HEAD_DIM].T
        for half in range(2):
            lhs[g, half, 0:HEAD_DIM, 0:BLK] = vt[:, half * BLK : (half + 1) * BLK]
    for g in range(KV_HEADS):
        scale = jnp.concatenate([to_end[g : g + 1], to_end[KV_HEADS + g : KV_HEADS + g + 1]], axis=1)
        keyed[g] = features_t(scores[g], scale).astype(BF16).T
    norms = []
    for g in range(KV_HEADS):
        left = jnp.concatenate([lhs[g, 0, :, 0:BLK], lhs[g, 1, :, 0:BLK]], axis=1)
        state = dot(left, keyed[g])
        norms.append(state[HEAD_DIM : HEAD_DIM + 1])
        for part in range(HEAD_DIM // rows):
            send1[g * (HEAD_DIM // rows) + part, 0:rows] = (
                state[part * rows : (part + 1) * rows].astype(BF16)
            )
    small = two_parts(jnp.concatenate(norms, axis=0), closing)
    for j in range(n_in):
        send1[j, rows:] = small
    loads[4].wait()
    pl.semaphore_wait(barrier, n_in - 1 + band)
    for k in range(n_in - 1, 0, -1):
        copy1(k).start()

    def tell_earlier(z, carry):
        pl.semaphore_signal(ready, inc=1, device_id={"outer": z}, device_id_type=MESH)
        return carry

    lax.fori_loop(0, band, tell_earlier, 0)

    @pl.when(band == 0)
    def _():
        for c in range(1, chips):
            map_copy(c).start()

    map_pass(0).start()
    recv1[me] = send1[me]
    for g in range(KV_HEADS):
        early[g] = dot(lhs[g, 0, :, 0:BLK], keyed[g, 0:BLK])
    for i in range(5, 8):
        loads[i].wait()
    mine = lax.div(me * rows, HEAD_DIM)
    prefix_t[...] = ps_ref[mine].T

    def run_pairs(pairs):
        def project(n):
            pair, places = pairs[n]
            for e in range(2):
                h = pair * 2 + e
                q = q_ref[:, pl.ds(pl.multiple_of(h * HEAD_DIM, HEAD_DIM), HEAD_DIM)]
                source, i = places[e]
                scores[2 * n + e] = dot_nt(maps[source, i], q)

        def soften(n):
            pair = pairs[n][0]
            for e in range(2):
                feat = features_t(scores[2 * n + e]).astype(BF16)
                at = slice(e * BLK, (e + 1) * BLK)
                rhs[pair, 0, BLK:, at] = feat[:, :BLK]
                rhs[pair, 1, BLK:, at] = feat[:, BLK:]

        def weigh(n):
            pair = pairs[n][0]
            g = lax.div(pair * 2, GROUP)
            for half in range(2):
                keys = keyed[g, half * BLK : (half + 1) * BLK]
                weights = dot(keys, rhs[pair, half, BLK:])
                rhs[pair, half, 0:BLK] = weights.astype(BF16) * mask[...]

        count = len(pairs)
        project(0)
        for n in range(count + 1):
            if n + 1 < count:
                project(n + 1)
            if n < count:
                soften(n)
            if n > 0:
                weigh(n - 1)

    def heads_of(place):
        run_pairs([
            (
                place * per + n,
                [(place * 2 + m // per, m % per) for m in (2 * n, 2 * n + 1)],
            )
            for n in range(per)
        ])

    def heads_from(sources):
        run_pairs([
            (source * (per // 2) + n, [(source, 2 * n), (source, 2 * n + 1)])
            for source in sources
            for n in range(per // 2)
        ])

    def heads_later(c, carry):
        map_pass(c).wait_recv()
        heads_of(lax.rem(chip - c + chips, chips))
        return carry

    def pass_on(c, carry):
        map_copy(c).wait_recv()
        map_pass(c).start()
        return carry

    map_pass(0).wait_recv()
    heads_of(chip)

    @pl.when(band > 0)
    def _():
        for c in range(1, chips):
            map_copy(c).start()


    all1().wait_recv()
    total = jnp.zeros((rows, FEATURES), F32)
    total_norm = jnp.zeros((KV_HEADS, FEATURES), F32)
    total_decay = jnp.ones((KV_HEADS, FEATURES), F32)
    total_lead = jnp.ones((1, FEATURES), F32)
    leads = []
    my_within = total_norm
    my_decay = total_decay
    for j in range(n_in):
        block, block_norm, decay, lead = unpacked(recv1, j, rows, mine)
        total, total_norm = lead * total, decay * total_norm
        total_lead, total_decay = lead * total_lead, decay * total_decay
        within[j] = total
        leads.append(total_lead)
        my_within = jnp.where(j == me, total_norm, my_within)
        my_decay = jnp.where(j == me, total_decay, my_decay)
        total, total_norm = total + block, total_norm + block_norm
    send2[0:rows] = total.astype(BF16)
    send2[rows:] = two_parts(total_norm, total_decay)

    @pl.when(band < n_out - 1)
    def _():
        pl.semaphore_wait(ready, n_out - 1 - band)

    def send_later(z, carry):
        copy2(band, z).start()
        return carry

    lax.fori_loop(band + 1, n_out, send_later, 0)

    def send_states(state):
        for j in range(n_in):
            send3[j] = (leads[j] * state + within[j]).astype(BF16)
        for k in range(n_in - 1, 0, -1):
            copy3(k).start()
        recv3[me] = send3[me]

    my_prefix = pl.ds(pl.multiple_of(lax.rem(me * rows, HEAD_DIM), rows), rows)

    @pl.when(band == 0)
    def _():
        send_states(prefix_t[my_prefix])

    lax.fori_loop(1, chips, pass_on, 0)

    def arrived(z, carry):
        copy2(z, z).wait_recv()
        return carry

    lax.fori_loop(0, band, arrived, 0)
    state = prefix_t[my_prefix]
    norm = pn_ref[...]
    for z in range(n_out - 1):
        before = z < band
        block, block_norm, decay, lead = unpacked(recv2, z, rows, mine)
        state = jnp.where(before, lead * state + block, state)
        norm = jnp.where(before, decay * norm + block_norm, norm)

    @pl.when(band > 0)
    def _():
        send_states(state)

    my_norm = my_decay * norm + my_within

    mid_norm = my_norm + jnp.concatenate(
        [early[g, HEAD_DIM : HEAD_DIM + 1] for g in range(KV_HEADS)], axis=0
    )
    pick = lax.broadcasted_iota(jnp.int32, (AUG - HEAD_DIM, FEATURES), 0)
    for half, entry in enumerate((my_norm, mid_norm)):
        high = entry.astype(BF16).astype(F32)
        low = entry - high
        for g in range(KV_HEADS):
            lhs[g, half, HEAD_DIM:, BLK:] = jnp.where(
                pick == 0, high[g : g + 1], jnp.where(pick == 1, low[g : g + 1], 0.0)
            ).astype(BF16)
    def finish_own():
        copy3(1).wait_recv()
        if chips == KV_HEADS:
            for part in range(2):
                at = slice(part * rows, (part + 1) * rows)
                entry = recv3[chip * 2 + part]
                lhs[chip, 0, at, BLK:] = entry
                lhs[chip, 1, at, BLK:] = (entry.astype(F32) + early[chip, at]).astype(BF16)
            for i in range(GROUP // 2):
                for half in range(2):
                    attend(
                        lhs[chip, half], rhs[chip * (GROUP // 2) + i, half],
                        done, half, i * 2 * HEAD_DIM,
                    )

    def heads_by_device():
        places = [lax.rem(chip - c + chips, chips) for c in range(1, chips)]
        heads_from([place * 2 + core for place in places])
        for c in range(1, chips):
            map_pass(c).wait_recv()
        heads_from([place * 2 + 1 - core for place in places])

    @pl.when(band == 0)
    def _():
        finish_own()
        lax.fori_loop(1, chips, heads_later, 0)

    @pl.when(band > 0)
    def _():
        if per % 2 == 0 and chips <= 4:
            heads_by_device()
        else:
            lax.fori_loop(1, chips, heads_later, 0)
        finish_own()

    far3().wait_recv()
    for j in range(n_in):
        g, at = divmod(j * rows, HEAD_DIM)
        entry = recv3[j]
        lhs[g, 0, at : at + rows, BLK:] = entry
        lhs[g, 1, at : at + rows, BLK:] = (
            entry.astype(F32) + early[g, at : at + rows]
        ).astype(BF16)

    all1().wait_send()
    all3().wait_send()
    all_maps().wait_send()

    def sent(z, carry):
        copy2(band, z).wait_send()
        return carry

    lax.fori_loop(band + 1, n_out, sent, 0)


def attend(left, right, out_ref, half, column):
    full = dot(left, right)
    den = full[HEAD_DIM : HEAD_DIM + 1] + full[HEAD_DIM + 1 : HEAD_DIM + 2]
    out = (full[:HEAD_DIM] * (1.0 / den)).astype(BF16)
    for i in range(2):
        at = column + i * HEAD_DIM
        out_ref[half * BLK : (half + 1) * BLK, at : at + HEAD_DIM] = (
            out[:, i * BLK : (i + 1) * BLK].T
        )


def finish(ready_made, rhs_ref, lhs_ref, done_ref, o_hbm, o_ref, drain, drain_done):
    wide = GROUP * HEAD_DIM
    left_over = KV_HEADS
    own = 0
    if ready_made:
        left_over = KV_HEADS - 1
        own = lax.div(lax.axis_index("inner"), 2)
        early_out = pltpu.make_async_copy(
            done_ref, o_hbm.at[:, pl.ds(pl.multiple_of(own * wide, wide), wide)], drain_done
        )
        early_out.start()
    for n in range(left_over):
        g = lax.rem(own + 1 + n, KV_HEADS)
        for i in range(GROUP // 2):
            column = n * wide + i * 2 * HEAD_DIM
            for half in range(2):
                attend(lhs_ref[g, half], rhs_ref[g * (GROUP // 2) + i, half], o_ref, half, column)
            target = pl.multiple_of(g * wide + i * 2 * HEAD_DIM, 2 * HEAD_DIM)
            pltpu.make_async_copy(
                o_ref.at[:, pl.ds(column, 2 * HEAD_DIM)],
                o_hbm.at[:, pl.ds(target, 2 * HEAD_DIM)], drain,
            ).start()
    pltpu.make_async_copy(
        o_ref.at[:, pl.ds(0, left_over * wide)], o_hbm.at[:, pl.ds(0, left_over * wide)], drain
    ).wait()
    if ready_made:
        early_out.wait()


def per_device(n_in, n_out, q, k, v, d, query_map, key_map, prefix_state, prefix_norm):
    args = (
        q, k, v, d, jnp.swapaxes(query_map, 1, 2), jnp.swapaxes(key_map, 1, 2),
        prefix_state, prefix_norm,
    )
    per = HEADS // n_in
    rows = KV_HEADS * HEAD_DIM // n_in
    dma = pltpu.SemaphoreType.DMA
    rhs, lhs, done = pl.pallas_call(
        functools.partial(kernel, n_in, n_out),
        out_shape=(
            pltpu.VMEM((PAIRS, 2, TOK, TOK), BF16),
            pltpu.VMEM((KV_HEADS, 2, AUG, TOK), BF16),
            pltpu.VMEM((TOK, GROUP * HEAD_DIM), BF16),
        ),
        in_specs=[pl.BlockSpec(memory_space=pltpu.HBM)] * 8,
        out_specs=(pl.BlockSpec(memory_space=pltpu.VMEM),) * 3,
        scratch_shapes=[
            pltpu.VMEM((TOK, HEADS * HEAD_DIM), BF16),
            pltpu.VMEM((TOK, KV_HEADS * HEAD_DIM), BF16),
            pltpu.VMEM((TOK, KV_HEADS * HEAD_DIM), BF16),
            pltpu.VMEM((KV_HEADS, TOK), F32),
            pltpu.VMEM((KV_HEADS, HALF, HEAD_DIM), BF16),
            pltpu.VMEM((KV_HEADS, FEATURES, HEAD_DIM), F32),
            pltpu.VMEM((KV_HEADS, FEATURES), F32),
            dma((8,)),
            pltpu.VMEM((n_in, per, HALF, HEAD_DIM), BF16),
            pltpu.VMEM((KV_HEADS, TOK, FEATURES), BF16),
            pltpu.VMEM((KV_HEADS, AUG, FEATURES), F32),
            pltpu.VMEM((BLK, TOK), BF16),
            pltpu.VMEM((max(4 * per, KV_HEADS), HALF, TOK), F32),
            pltpu.VMEM((HEAD_DIM, FEATURES), F32),
            pltpu.VMEM((n_in, rows, FEATURES), F32),
            pltpu.VMEM((n_in, rows + 16, FEATURES), BF16),
            pltpu.VMEM((n_in, rows + 16, FEATURES), BF16),
            pltpu.VMEM((rows + 16, FEATURES), BF16),
            pltpu.VMEM((n_out, rows + 16, FEATURES), BF16),
            pltpu.VMEM((n_in, rows, FEATURES), BF16),
            pltpu.VMEM((n_in, rows, FEATURES), BF16),
            dma(()), dma((n_in,)), dma(()), dma(()),
            dma((n_out,)), dma((n_out,)), dma(()), dma(()), dma(()),
            pltpu.SemaphoreType.REGULAR,
        ],
        compiler_params=pltpu.CompilerParams(
            collective_id=0, has_side_effects=True, vmem_limit_bytes=57 << 20
        ),
    )(*args)
    return pl.pallas_call(
        functools.partial(finish, n_in // 2 == KV_HEADS),
        out_shape=jax.ShapeDtypeStruct((TOK, HEADS * HEAD_DIM), BF16),
        in_specs=[pl.BlockSpec(memory_space=pltpu.VMEM)] * 3,
        out_specs=pl.BlockSpec(memory_space=pltpu.HBM),
        scratch_shapes=[
            pltpu.VMEM((TOK, HEADS * HEAD_DIM), BF16),
            dma(()), dma(()),
        ],
        compiler_params=pltpu.CompilerParams(vmem_limit_bytes=24 << 20),
    )(rhs, lhs, done)


def solution(mesh):
    placed = (
        P(("outer", "inner"), None),
        P(("outer", "inner"), None),
        P(("outer", "inner"), None),
        P(None, ("outer", "inner")),
        P("inner", None, None),
        P(),
        P(),
        P(),
    )
    return jax.shard_map(
        functools.partial(per_device, mesh.shape["inner"], mesh.shape["outer"]),
        mesh=mesh,
        in_specs=placed,
        out_specs=P(("outer", "inner"), None),
        check_vma=False,
    )
```
